128 devices in a mesh: row: 8 (over y, core), col: 16 (over x, z).
Axes of the slice: x: 4, y: 4, z: 4, core: 2. Of those that a mesh axis runs over, the one named last changes fastest.
Arguments:
- user_emb: float32 [8, 16, 2048, 128], P('row', 'col'), may hold values from -2.4 to 2.4
- item_emb: float32 [16, 8, 1024, 128], P('col', 'row'), may hold values from -2.4 to 2.4
- tile_vals: bfloat16 [8, 16, 512, 128, 128], P('row', 'col'), may hold values from 0 to 0.029907227
- tile_rows: int32 [8, 16, 512], P('row', 'col'), may hold values from 0 to 255
- tile_cols: int32 [8, 16, 512], P('row', 'col'), may hold values from 0 to 63
- tile_count: int32 [8, 16], P('row', 'col'), may hold values from 128 to 512, as said below
- pair_users: int32 [65536], P(('row', 'col')), may hold values from 0 to 262143, as said below
- pair_items: int32 [65536], P(('row', 'col')), may hold values from 0 to 131071, as said below
- negatives: int32 [1024], replicated, may hold values from 0 to 131071, as said below
Outputs:
- user_final: float32 [8, 16, 2048, 128], P('row', 'col')
- item_final: float32 [16, 8, 1024, 128], P('col', 'row')
- bpr_terms: float32 [65536, 1024], P(('row', 'col'))
The draws below stay inside these ranges and needn't reach their ends.
Inputs may be any that keep to these rules, and one draw needn't show every extreme that they name: `pair_users`: taken in aligned blocks of 512 entries, at most 8 entries of one block name users that one device holds in user_emb; in every draw some device's users are named exactly 8 times in every block. `pair_items`: taken in aligned blocks of 512 entries, at most 8 entries of one block name items that one device holds in item_emb; in every draw some device's items are named exactly 8 times in every block. `tile_count`: some block has all 512 slots live. `negatives`: entry j names an item that the device with row index (j // 8) // 16 and col index (j // 8) % 16 holds in item_emb.
All inputs are finite; a program needn't handle non-finite values.
Results may differ from the reference program's by a relative error of at most 0.009.
Values may be sent and summed in bfloat16 or wider, within the bound.
A program may use at most 128 MiB of HBM per device.

```python
import jax
import jax.numpy as jnp
from jax import lax

E = 128
TILE = 128
UDEV = 2048
IDEV = 1024
TILES_DEV = 512
PAIRS_DEV = 512
NEG = 1024
PAIRS = 65536
TROWS = 256
TCOLS = 64
N_ROW = 8
N_COL = 16


def owner_blocks(key):
    devices = N_ROW * N_COL
    common = jax.random.randint(jax.random.fold_in(key, 1), (), 0, devices)

    def one_block(subkey):
        first, second = jax.random.split(subkey)
        emptied = (common + jax.random.randint(first, (), 1, devices)) % devices
        owners = jnp.arange(PAIRS_DEV, dtype=jnp.int32) % devices
        owners = jnp.where(owners == emptied, common, owners)
        return jax.random.permutation(second, owners)
    subkeys = jax.random.split(jax.random.fold_in(key, 2), devices)
    return jax.vmap(one_block)(subkeys).reshape(-1)


def draw_pair_users(key, part):
    owners = owner_blocks(jax.random.fold_in(key, 11))
    local = jax.random.randint(jax.random.fold_in(key, 12), (PAIRS,), 0, UDEV)
    return (owners * UDEV + local).astype(jnp.int32)


def draw_pair_items(key, part):
    owners = owner_blocks(jax.random.fold_in(key, 21))
    local = jax.random.randint(jax.random.fold_in(key, 22), (PAIRS,), 0, IDEV)
    holder = owners % N_COL * N_ROW + owners // N_COL
    return (holder * IDEV + local).astype(jnp.int32)


def draw_tile_count(key, part):
    counts = jax.random.randint(jax.random.fold_in(key, 31), (N_ROW * N_COL,), TILES_DEV // 4, TILES_DEV + 1)
    chosen = jax.random.randint(jax.random.fold_in(key, 32), (), 0, N_ROW * N_COL)
    counts = counts.at[chosen].set(TILES_DEV)
    return counts.reshape(N_ROW, N_COL).astype(jnp.int32)


def draw_negatives(key, part):
    per_device = NEG // (N_ROW * N_COL)
    device = jnp.arange(NEG, dtype=jnp.int32) // per_device
    holder = device % N_COL * N_ROW + device // N_COL
    local = jax.random.randint(jax.random.fold_in(key, 41), (NEG,), 0, IDEV)
    return (holder * IDEV + local).astype(jnp.int32)


def set_ends(array, own_key, least, high):
    longest = array.shape.index(max(array.shape))
    spots = []
    for shift in (0, 1):
        where = [jax.random.randint(jax.random.fold_in(own_key, axis), (), 0, length) for axis, length in enumerate(array.shape)]
        where[longest] = (where[longest] + shift) % array.shape[longest]
        spots.append(tuple(where))
    return array.at[spots[0]].set(least).at[spots[1]].set(high)


def steps_of(stream_key, extent, cuts, least, top_value):
    level, own = 1.0, jax.random.fold_in(stream_key, 6)
    for position, blocks in cuts:
        steps = jnp.exp(jax.random.uniform(jax.random.fold_in(own, position), (blocks,), jnp.float32, least / len(cuts), top_value / len(cuts)))
        level = level * jnp.repeat(steps, extent[position] // blocks).reshape([-1 if axis == position else 1 for axis in range(len(extent))])
    return level


def bell_draw(rng, dims, scale, limit, shards=(), kind=jnp.bfloat16):
    result = scale * jax.random.normal(rng, dims, jnp.float32)
    if shards:
        result = result * steps_of(rng, dims, shards, -0.22, 0.18)
    return jnp.clip(result, -limit, limit).astype(kind)


def setup_inputs(seed: int = 0) -> dict:
    seeds = jax.random.split(jax.random.key(seed), 10)
    user_emb = bell_draw(seeds[0], (N_ROW, N_COL, UDEV, E), 0.4, 2.4, ((0, 8), (1, 16)), jnp.float32)
    item_emb = bell_draw(seeds[1], (N_COL, N_ROW, IDEV, E), 0.4, 2.4, ((0, 16), (1, 8)), jnp.float32)
    tile_vals = jnp.clip(0.029907227 * jax.random.uniform(seeds[2], (N_ROW, N_COL, TILES_DEV, TILE, TILE), jnp.float32) ** steps_of(seeds[2], (N_ROW, N_COL, TILES_DEV, TILE, TILE), ((0, 8), (1, 16)), -0.2, 0.2), 0.0, 0.029907227).astype(jnp.bfloat16)
    tile_rows = set_ends(jax.random.randint(seeds[3], (N_ROW, N_COL, TILES_DEV), 0, TROWS), jax.random.fold_in(seeds[3], 1), 0, TROWS - 1).astype(jnp.int32)
    tile_cols = set_ends(jax.random.randint(seeds[4], (N_ROW, N_COL, TILES_DEV), 0, TCOLS), jax.random.fold_in(seeds[4], 1), 0, TCOLS - 1).astype(jnp.int32)
    tile_count = draw_tile_count(jax.random.fold_in(seeds[9], 71), 0)
    pair_users = draw_pair_users(jax.random.fold_in(seeds[9], 71), 0)
    pair_items = draw_pair_items(jax.random.fold_in(seeds[9], 71), 0)
    negatives = draw_negatives(jax.random.fold_in(seeds[9], 71), 0)
    return dict(user_emb=user_emb, item_emb=item_emb, tile_vals=tile_vals, tile_rows=tile_rows, tile_cols=tile_cols, tile_count=tile_count, pair_users=pair_users, pair_items=pair_items, negatives=negatives)


def rounded(values):
    return lax.optimization_barrier(values.astype(jnp.bfloat16)).astype(jnp.float32)


def reference(user_emb, item_emb, tile_vals, tile_rows, tile_cols, tile_count, pair_users, pair_items, negatives):
    user_low = rounded(user_emb)
    item_low = rounded(item_emb)
    row_tiles = N_COL * UDEV // TILE
    col_tiles = N_ROW * IDEV // TILE

    def visit(totals, device):
        user_prop, item_prop = totals
        row_block = device // N_COL
        col_block = device % N_COL
        values = tile_vals[row_block, col_block].astype(jnp.float32)
        row_ids = tile_rows[row_block, col_block]
        col_ids = tile_cols[row_block, col_block]
        live = (jnp.arange(TILES_DEV, dtype=jnp.int32) < tile_count[row_block, col_block]).astype(jnp.float32)[:, None, None]
        user_tiles = user_low[row_block].reshape(row_tiles, TILE, E)
        item_tiles = item_low[col_block].reshape(col_tiles, TILE, E)
        to_users = jnp.einsum("tij,tje->tie", values, item_tiles[col_ids]) * live
        to_items = jnp.einsum("tij,tie->tje", values, user_tiles[row_ids]) * live
        user_add = rounded(jnp.zeros((row_tiles, TILE, E), jnp.float32).at[row_ids].add(to_users))
        item_add = rounded(jnp.zeros((col_tiles, TILE, E), jnp.float32).at[col_ids].add(to_items))
        user_prop = user_prop.at[row_block].add(user_add.reshape(N_COL, UDEV, E))
        item_prop = item_prop.at[col_block].add(item_add.reshape(N_ROW, IDEV, E))
        return (user_prop, item_prop), None

    start = (jnp.zeros(user_emb.shape, jnp.float32), jnp.zeros(item_emb.shape, jnp.float32))
    (user_prop, item_prop), _ = lax.scan(visit, start, jnp.arange(N_ROW * N_COL, dtype=jnp.int32))
    user_final = (user_emb + user_prop) * 0.5
    item_final = (item_emb + item_prop) * 0.5
    user_flat = user_final.reshape(-1, E)
    item_flat = item_final.reshape(-1, E)
    user_vec = user_flat[pair_users]
    item_vec = item_flat[pair_items]
    negative_vec = item_flat[negatives]
    positive = jnp.sum(user_vec * item_vec, axis=1)
    against = jnp.dot(user_vec, negative_vec.T, precision=lax.Precision.HIGHEST)
    bpr_terms = jnp.log1p(jnp.exp(against - positive[:, None]))
    return user_final, item_final, bpr_terms
```

```python
import functools

import jax
import jax.numpy as jnp
from jax import lax
from jax.experimental import pallas as pl
from jax.experimental.pallas import tpu as pltpu
from jax.sharding import Mesh
from jax.sharding import PartitionSpec as P

ROW = ("row_0", "row_1")
COL = ("col_0", "col_1")
ROW_COL = ("row_0", "row_1", "col_0", "col_1")


def from_everyone(array, axis):
    copies = jnp.broadcast_to(array, (lax.axis_size(axis), *array.shape))
    return lax.all_to_all(copies, axis, split_axis=0, concat_axis=0, tiled=True)


def in_order(blocks, dim):
    blocks = jnp.moveaxis(blocks, 0, dim)
    shape = blocks.shape
    return blocks.reshape(*shape[:dim], shape[dim] * shape[dim + 1], *shape[dim + 2 :])


def collect(array, axis, dim):
    blocks = from_everyone(array, axis)
    return in_order(blocks, dim)


def in_blocks(array, dim, length):
    shape = array.shape
    blocks = array.reshape(*shape[:dim], length, shape[dim] // length, *shape[dim + 1 :])
    return jnp.moveaxis(blocks, dim, 0)


def sent_and_summed(array, axis, dim):
    blocks = in_blocks(array, dim, lax.axis_size(axis))
    arrived = lax.all_to_all(blocks, axis, split_axis=0, concat_axis=0, tiled=True)
    return arrived.astype(jnp.float32).sum(axis=0)


def gather_in_order(array, axes, sequence):
    blocks = array[None]
    for k in sequence:
        blocks = lax.all_gather(blocks, axes[k], axis=0, tiled=True)
    held = [lax.axis_size(axes[k]) for k in reversed(sequence)]
    blocks = blocks.reshape(*held, *array.shape)
    turned = sorted(range(len(sequence)), key=lambda place: sequence[len(sequence) - 1 - place])
    return blocks.transpose(*turned, *range(len(sequence), blocks.ndim)).reshape(-1, *array.shape)


def whole_of(array, axes, sequence, dim):
    return in_order(gather_in_order(array, axes, sequence), dim)


def tile_kernel(width, depth, users, count_ref, rows, cols, vals, table, out, acc, bufs, sems):
    total = out.shape[0]
    count = count_ref[0]
    chunks = (count + width - 1) // width

    def fetch(k, slot):
        return pltpu.make_async_copy(vals.at[pl.ds(k * width, width)], bufs.at[slot], sems.at[slot])

    for k in range(depth - 1):

        @pl.when(k < chunks)
        def _():
            fetch(k, k).start()

    @pl.loop(0, total + 1)
    def _(i):
        acc[i] = jnp.zeros(acc.shape[1:], jnp.float32)

    @pl.loop(0, chunks)
    def _(k):
        slot = lax.rem(k, depth)
        ahead = k + depth - 1

        @pl.when(ahead < chunks)
        def _():
            fetch(ahead, lax.rem(ahead, depth)).start()

        fetch(k, slot).wait()
        products = []
        for t in range(width):
            spot = k * width + t
            tile = bufs[slot, t]
            if users:
                left, right, place = tile, table[cols[spot]], rows[spot]
            else:
                left, right, place = table[rows[spot]], tile, cols[spot]
            product = jnp.dot(left, right, preferred_element_type=jnp.float32)
            products.append((jnp.where(spot < count, place, total), product))
        for place, product in products:
            acc[place] += product

    @pl.loop(0, total)
    def _(i):
        tile = acc[i]
        out[i] = (tile if users else tile.T).astype(jnp.bfloat16)


def tile_terms(users, vals, rows, cols, count, table, total, width=16, depth=3):
    slots, side, embed = *vals.shape[:2], table.shape[-1]
    smem = pl.BlockSpec(memory_space=pltpu.SMEM)
    vmem = pl.BlockSpec(memory_space=pltpu.VMEM)
    return pl.pallas_call(
        functools.partial(tile_kernel, width, depth, users),
        name="user_terms" if users else "item_terms",
        out_shape=jax.ShapeDtypeStruct((total, side, embed), jnp.bfloat16),
        in_specs=[smem, smem, smem, pl.BlockSpec(memory_space=pl.ANY), vmem],
        out_specs=vmem,
        scratch_shapes=[
            pltpu.VMEM((total + 1, side, embed), jnp.float32),
            pltpu.VMEM((depth, width, side, side), jnp.bfloat16),
            pltpu.SemaphoreType.DMA((depth,)),
        ],
        compiler_params=pltpu.CompilerParams(vmem_limit_bytes=56 * 2**20),
        cost_estimate=pl.CostEstimate(
            flops=slots * 2 * side * side * embed,
            bytes_accessed=2 * (vals.size + table.size + total * side * embed),
            transcendentals=0,
        ),
    )(count, rows, cols, vals, table)


def place_requests(owner, local, devices, slots_per):
    hits = (owner[:, None] == jnp.arange(devices, dtype=jnp.int32)[None, :]).astype(jnp.int32)
    rank = jnp.sum((jnp.cumsum(hits, axis=0) - 1) * hits, axis=1)
    slot = owner * slots_per + rank
    request = jnp.zeros((devices * slots_per,), jnp.int32).at[slot].set(local)
    return (slot, request.reshape(devices, slots_per))


def on_device(
    user_emb,
    item_emb,
    tile_vals,
    tile_rows,
    tile_cols,
    tile_count,
    pair_users,
    pair_items,
    negatives,
):
    row_count = lax.axis_size(ROW)
    col_count = lax.axis_size(COL)
    user_dev = user_emb.shape[2]
    item_dev = item_emb.shape[2]
    embed = user_emb.shape[3]
    tile_side = tile_vals.shape[-1]
    user_turned = user_emb[0, 0].reshape(-1, tile_side, embed).swapaxes(1, 2)
    user_tiles = lax.all_gather(user_turned.astype(jnp.bfloat16), COL, axis=0, tiled=True)
    item_whole = collect(item_emb.astype(jnp.bfloat16), ROW, 1)
    item_tiles = item_whole.reshape(-1, tile_side, embed)
    slots = (tile_vals[0, 0], tile_rows[0, 0], tile_cols[0, 0], tile_count[0])
    user_part = tile_terms(True, *slots, item_tiles, user_tiles.shape[0])
    item_part = tile_terms(False, *slots, user_tiles, item_tiles.shape[0])
    user_prop = lax.psum_scatter(
        user_part.reshape(-1, embed), COL, scatter_dimension=0, tiled=True
    ).astype(jnp.float32)
    item_prop = sent_and_summed(item_part.reshape(-1, embed), ROW, 0)
    user_final = (user_emb[0, 0] + user_prop) * 0.5
    item_final = (item_emb[0, 0] + item_prop) * 0.5
    devices = row_count * col_count
    slots_per = 2 * pair_users.shape[0] // devices
    user_owner = pair_users // user_dev
    user_local = pair_users % user_dev
    item_holder = pair_items // item_dev
    item_owner = item_holder % row_count * col_count + item_holder // row_count
    item_local = pair_items % item_dev
    user_slot, user_request = place_requests(user_owner, user_local, devices, slots_per)
    item_slot, item_request = place_requests(item_owner, item_local, devices, slots_per)
    user_wanted = lax.all_to_all(user_request, ROW_COL, split_axis=0, concat_axis=0, tiled=True)
    item_wanted = lax.all_to_all(item_request, ROW_COL, split_axis=0, concat_axis=0, tiled=True)
    user_rows = lax.all_to_all(
        user_final[user_wanted].astype(jnp.bfloat16),
        ROW_COL,
        split_axis=0,
        concat_axis=0,
        tiled=True,
    ).astype(jnp.float32)
    item_rows = lax.all_to_all(
        item_final[item_wanted].astype(jnp.bfloat16),
        ROW_COL,
        split_axis=0,
        concat_axis=0,
        tiled=True,
    ).astype(jnp.float32)
    user_vec = user_rows.reshape(-1, embed)[user_slot]
    item_vec = item_rows.reshape(-1, embed)[item_slot]
    offset = (lax.axis_index(COL) * row_count + lax.axis_index(ROW)) * item_dev
    neg_each = negatives.shape[0] // devices
    device_rank = lax.axis_index(ROW) * col_count + lax.axis_index(COL)
    mine = lax.dynamic_slice_in_dim(negatives, device_rank * neg_each, neg_each, 0) - offset
    negative_vec = whole_of(item_final[mine], ROW_COL, (0, 2, 3, 1), 0)
    positive = jnp.sum(user_vec * item_vec, axis=1)
    against = jnp.dot(user_vec, negative_vec.T, precision=lax.Precision.HIGHEST)
    bpr_terms = jnp.log1p(jnp.exp(against - positive[:, None]))
    return (user_final.reshape(user_emb.shape), item_final.reshape(item_emb.shape), bpr_terms)


def solution(mesh):
    torus = Mesh(mesh.devices.reshape(4, 2, 4, 4), ("row_0", "row_1", "col_0", "col_1"))
    return jax.shard_map(
        on_device,
        mesh=torus,
        in_specs=(
            P(ROW, COL, None, None),
            P(COL, ROW, None, None),
            P(ROW, COL, None, None, None),
            P(ROW, COL, None),
            P(ROW, COL, None),
            P(ROW, COL),
            P(ROW_COL),
            P(ROW_COL),
            P(),
        ),
        out_specs=(P(ROW, COL, None, None), P(COL, ROW, None, None), P(ROW_COL, None)),
        check_vma=False,
    )
```

```python
import functools

import jax
import jax.numpy as jnp
from jax import lax
from jax.experimental import pallas as pl
from jax.experimental.pallas import tpu as pltpu
from jax.sharding import Mesh
from jax.sharding import PartitionSpec as P

ROW = ("row_0", "row_1")
COL = ("col_0", "col_1")
Y, CORE, X, Z = "row_0", "row_1", "col_0", "col_1"
SIDE = 4
ANY = pl.BlockSpec(memory_space=pl.ANY)
VMEM = pl.BlockSpec(memory_space=pltpu.VMEM)
SMEM = pl.BlockSpec(memory_space=pltpu.SMEM)
DMA = pltpu.SemaphoreType.DMA
ROW_COL = ("row_0", "row_1", "col_0", "col_1")


def greet(peers):
    barrier = pltpu.get_barrier_semaphore()
    for peer in peers:
        pl.semaphore_signal(barrier, inc=1, device_id=peer)
    pl.semaphore_wait(barrier, len(peers))


def ahead(axis, step):
    return lax.rem(lax.axis_index(axis) + step, SIDE)


def first_gather_kernel(items, users, items_out, x_out, z_out, sent, came, kept):
    y, core, x, z = (lax.axis_index(a) for a in (Y, CORE, X, Z))
    shard, half = items.shape[0], users.shape[0] // 2
    other = {CORE: 1 - core}
    steps = range(1, SIDE)
    greet([other] + [{a: ahead(a, s)} for a in (Y, X, Z) for s in steps])

    def place(y_of, core_of):
        return items_out.at[pl.ds((y_of * 2 + core_of) * shard, shard)]

    def send(k, src, dst, peer):
        copy = pltpu.make_async_remote_copy(src, dst, sent.at[k], came.at[k], device_id=peer)
        copy.start()
        return copy

    copies = []
    to_y = [send(s - 1, items, place(y, core), {Y: ahead(Y, s)}) for s in steps]
    copies.append(send(3, items, place(y, core), other))
    for s in steps:
        copies.append(send(6 + s, users.at[pl.ds(0, half)], x_out.at[x], {X: ahead(X, s)}))
        copies.append(send(9 + s, users.at[pl.ds(half, half)], z_out.at[z], {Z: ahead(Z, s)}))
    local = [
        pltpu.make_async_copy(items, place(y, core), kept.at[0]),
        pltpu.make_async_copy(users.at[pl.ds(0, half)], x_out.at[x], kept.at[1]),
        pltpu.make_async_copy(users.at[pl.ds(half, half)], z_out.at[z], kept.at[2]),
    ]
    for copy in local:
        copy.start()
    for s in steps:
        to_y[s - 1].wait()
        back = lax.rem(y + SIDE - s, SIDE)
        copies.append(send(3 + s, place(back, core), place(back, core), other))
    for copy in copies + local:
        copy.wait()


def first_gather(items, users):
    side = items.shape[1:]
    half = users.shape[0] // 2
    stage = jax.ShapeDtypeStruct((SIDE, half, *side), jnp.bfloat16)
    return pl.pallas_call(
        first_gather_kernel,
        name="first_gather",
        out_shape=(jax.ShapeDtypeStruct((8 * items.shape[0], *side), jnp.bfloat16), stage, stage),
        in_specs=[ANY, ANY],
        out_specs=(ANY, ANY, ANY),
        scratch_shapes=[DMA((13,)), DMA((13,)), DMA((3,))],
        compiler_params=pltpu.CompilerParams(
            collective_id=0, has_side_effects=True, vmem_limit_bytes=2**20
        ),
    )(items, users)


def shifted(array, axis, step):
    return lax.ppermute(array, axis, [(i, (i + step) % SIDE) for i in range(SIDE)])


def settle_kernel(
    users, items, user_emb, item_emb, user_out, item_out,
    own_x, own_z, in_x, in_z, sum_x, sum_z, last_x, last_z, in_i, sent, came, kept,
):
    y, core, x, z = (lax.axis_index(a) for a in (Y, CORE, X, Z))
    steps = range(1, SIDE)
    half, shard = own_x.shape[1], in_i.shape[1]
    mates = [(s, c) for s in range(SIDE) for c in range(2) if s or c]

    def mate(s, c):
        return {Y: ahead(Y, s), CORE: lax.rem(core + c, 2)}

    greet([{a: ahead(a, s)} for a in (X, Z) for s in steps] + [mate(s, c) for s, c in mates])

    def send(k, src, dst, peer):
        copy = pltpu.make_async_remote_copy(src, dst, sent.at[k], came.at[k], device_id=peer)
        copy.start()
        return copy

    over_x = [send(s - 1, users.at[ahead(X, s), :, 0], in_x.at[s - 1], {X: ahead(X, s)}) for s in steps]
    over_z = [send(s + 2, users.at[:, ahead(Z, s), 1], in_z.at[s - 1], {Z: ahead(Z, s)}) for s in steps]
    keep = [
        pltpu.make_async_copy(users.at[x, :, 0], own_x, kept.at[0]),
        pltpu.make_async_copy(users.at[:, z, 1], own_z, kept.at[1]),
    ]
    for copy in keep:
        copy.start()
    over_i = []
    for k, (s, c) in enumerate(mates):
        goal = mate(s, c)
        rows = pl.ds((goal[Y] * 2 + goal[CORE]) * shard, shard)
        over_i.append(send(12 + k, items.at[rows], in_i.at[k], goal))

    def add_up(parts, to):
        @pl.loop(0, half)
        def _(i):
            total = parts[0][i].astype(jnp.float32)
            for part in parts[1:]:
                total += part[i].astype(jnp.float32)
            to[i] = total.astype(to.dtype)

    last = []
    for first, own, came_in, total, final, axis, base in (
        (over_x, own_x, in_x, sum_x, last_x, Z, 6),
        (over_z, own_z, in_z, sum_z, last_z, X, 9),
    ):
        keep[0 if axis == Z else 1].wait()
        for copy in first:
            copy.wait()
        for s in (1, 2, 3, 0):
            goal = ahead(axis, s)
            add_up([own.at[goal]] + [came_in.at[j, goal] for j in range(3)], total.at[goal])
            if s:
                last.append(send(base + s - 1, total.at[goal], final.at[s - 1], {axis: goal}))

    def finish(emb, to, start, count, parts):
        @pl.loop(0, count)
        def _(i):
            total = parts[0][i].astype(jnp.float32)
            for part in parts[1:]:
                total += part[i].astype(jnp.float32)
            to[start + i] = (emb[start + i] + total) * 0.5

    mine = pltpu.make_async_copy(items.at[pl.ds((y * 2 + core) * shard, shard)], in_i.at[7], kept.at[2])
    mine.start()
    for copy in over_i:
        copy.wait()
    mine.wait()
    finish(item_emb, item_out, 0, shard, [in_i.at[k] for k in range(8)])
    for copy in last[:3]:
        copy.wait()
    finish(user_emb, user_out, 0, half, [sum_x.at[z]] + [last_x.at[j] for j in range(3)])
    for copy in last[3:]:
        copy.wait()
    finish(user_emb, user_out, half, half, [sum_z.at[x]] + [last_z.at[j] for j in range(3)])


def settle(users, items, user_emb, item_emb):
    side = items.shape[1:]
    half, shard = user_emb.shape[0] // 2, item_emb.shape[0]
    users = users.reshape(SIDE, SIDE, 2, half, *side)
    many, one = (SIDE, half, *side), (half, *side)
    low = jnp.bfloat16
    return pl.pallas_call(
        settle_kernel,
        name="settle",
        out_shape=(
            jax.ShapeDtypeStruct(user_emb.shape, jnp.float32),
            jax.ShapeDtypeStruct(item_emb.shape, jnp.float32),
        ),
        in_specs=[ANY, ANY, VMEM, VMEM],
        out_specs=(VMEM, VMEM),
        scratch_shapes=[
            pltpu.VMEM(many, low), pltpu.VMEM(many, low),
            pltpu.VMEM((3, *many), low), pltpu.VMEM((3, *many), low),
            pltpu.VMEM(many, low), pltpu.VMEM(many, low),
            pltpu.VMEM((3, *one), low), pltpu.VMEM((3, *one), low),
            pltpu.VMEM((8, shard, *side), low),
            DMA((19,)), DMA((19,)), DMA((3,)),
        ],
        compiler_params=pltpu.CompilerParams(
            collective_id=1, has_side_effects=True, vmem_limit_bytes=58 * 2**20
        ),
    )(users, items, user_emb, item_emb)


def coords(rank):
    return {Y: rank // 32, CORE: lax.rem(rank // 16, 2), X: lax.rem(rank // 4, 4), Z: lax.rem(rank, 4)}


def exchange_kernel(
    devices, wanted_users, wanted_items, wanted_negatives, user_final, item_final, user_slot, item_slot,
    user_vec, positive, negative_vec, stage, packs, arrived, sent, came, kept,
):
    me = ((lax.axis_index(Y) * 2 + lax.axis_index(CORE)) * 4 + lax.axis_index(X)) * 4 + lax.axis_index(Z)
    barrier = pltpu.get_barrier_semaphore()

    def other(s):
        return lax.rem(me + s, devices)

    @pl.loop(1, devices)
    def _(s):
        pl.semaphore_signal(barrier, inc=1, device_id=coords(other(s)))

    each = wanted_negatives.shape[0]
    for k in range(each):
        stage[pl.ds(2 * each + k, 1)] = item_final[pl.ds(wanted_negatives[k], 1)]
    negs = stage[pl.ds(2 * each, each)]

    @pl.loop(0, devices)
    def _(d):
        for k in range(each):
            stage[pl.ds(k, 1)] = user_final[pl.ds(wanted_users[d * each + k], 1)]
            stage[pl.ds(each + k, 1)] = item_final[pl.ds(wanted_items[d * each + k], 1)]
        packs[d] = stage[...].astype(jnp.bfloat16)

    pl.semaphore_wait(barrier, devices - 1)

    def message(s):
        return pltpu.make_async_remote_copy(
            packs.at[other(s)], arrived.at[me], sent, came, device_id=coords(other(s))
        )

    @pl.loop(1, devices)
    def _(s):
        message(s).start()

    mine = pltpu.make_async_copy(packs.at[me], arrived.at[me], kept)
    mine.start()
    rest = pl.ds(0, devices - 1)
    mine.wait()
    pltpu.make_async_copy(packs.at[rest], arrived.at[rest], came).wait()
    pltpu.make_async_copy(packs.at[rest], arrived.at[rest], sent).wait()

    def picked(slot, first):
        rows = arrived[:, pl.ds(first, each)].reshape(devices * each, -1)
        hits = lax.broadcasted_iota(jnp.int32, (slot.shape[0], devices * each), 1) == slot[...]
        return jnp.dot(hits.astype(jnp.bfloat16), rows, preferred_element_type=jnp.float32)

    users = picked(user_slot, 0)
    items = picked(item_slot, each)
    positive[...] = jnp.sum(users * items, axis=1, keepdims=True)
    user_vec[...] = users.astype(jnp.bfloat16)
    negative_vec[...] = arrived[:, pl.ds(2 * each, each)].reshape(devices * each, -1)


def exchange(wanted_users, wanted_items, wanted_negatives, user_final, item_final, user_slot, item_slot):
    embed = user_final.shape[-1]
    each = wanted_negatives.shape[0]
    devices, pairs = wanted_users.shape[0] // each, user_slot.shape[0]
    low = jnp.bfloat16
    return pl.pallas_call(
        functools.partial(exchange_kernel, devices),
        name="exchange",
        out_shape=(
            jax.ShapeDtypeStruct((pairs, embed), low),
            jax.ShapeDtypeStruct((pairs, 1), jnp.float32),
            jax.ShapeDtypeStruct((devices * each, embed), low),
        ),
        in_specs=[SMEM, SMEM, SMEM, VMEM, VMEM, VMEM, VMEM],
        out_specs=(VMEM, VMEM, VMEM),
        scratch_shapes=[
            pltpu.VMEM((3 * each, embed), jnp.float32),
            pltpu.VMEM((devices, 3 * each, embed), low),
            pltpu.VMEM((devices, 3 * each, embed), low),
            DMA, DMA, DMA,
        ],
        compiler_params=pltpu.CompilerParams(
            collective_id=2, has_side_effects=True, vmem_limit_bytes=32 * 2**20
        ),
    )(wanted_users, wanted_items, wanted_negatives, user_final, item_final, user_slot, item_slot)


def tile_kernel(width, depth, users, place, pieces, count_ref, rows, cols, vals, *refs):
    parts, (out, acc, bufs, table, sems, filled) = refs[:pieces], refs[pieces:]
    total = out.shape[0]
    count = count_ref[0]
    chunks = (count + width - 1) // width

    def fetch(k, slot):
        return pltpu.make_async_copy(vals.at[pl.ds(k * width, width)], bufs.at[slot], sems.at[slot])

    for k in range(depth - 1):

        @pl.when(k < chunks)
        def _():
            fetch(k, k).start()

    copies = [
        pltpu.make_async_copy(part, table.at[pl.ds(start, part.shape[0])], filled)
        for part, start in place(parts)
    ]
    for copy in copies:
        copy.start()

    @pl.loop(0, total + 1)
    def _(i):
        acc[i] = jnp.zeros(acc.shape[1:], jnp.float32)

    pltpu.make_async_copy(table, table, filled).wait()

    @pl.loop(0, chunks)
    def _(k):
        slot = lax.rem(k, depth)
        ahead = k + depth - 1

        @pl.when(ahead < chunks)
        def _():
            fetch(ahead, lax.rem(ahead, depth)).start()

        fetch(k, slot).wait()
        products = []
        for t in range(width):
            spot = k * width + t
            tile = bufs[slot, t]
            if users:
                left, right, goal = tile, table[cols[spot]], rows[spot]
            else:
                left, right, goal = table[rows[spot]], tile, cols[spot]
            product = jnp.dot(left, right, preferred_element_type=jnp.float32)
            products.append((jnp.where(spot < count, goal, total), product))
        for goal, product in products:
            acc[goal] += product

    @pl.loop(0, total)
    def _(i):
        tile = acc[i]
        out[i] = (tile if users else tile.T).astype(jnp.bfloat16)


def tile_terms(users, vals, rows, cols, count, parts, place, held, total, width=16, depth=3):
    slots, side, embed = *vals.shape[:2], parts[0].shape[-1]
    return pl.pallas_call(
        functools.partial(tile_kernel, width, depth, users, place, len(parts)),
        name="user_terms" if users else "item_terms",
        out_shape=jax.ShapeDtypeStruct((total, side, embed), jnp.bfloat16),
        in_specs=[SMEM, SMEM, SMEM, ANY] + [ANY] * len(parts),
        out_specs=VMEM,
        scratch_shapes=[
            pltpu.VMEM((total + 1, side, embed), jnp.float32),
            pltpu.VMEM((depth, width, side, side), jnp.bfloat16),
            pltpu.VMEM((held, side, embed), jnp.bfloat16),
            DMA((depth,)),
            DMA,
        ],
        compiler_params=pltpu.CompilerParams(vmem_limit_bytes=56 * 2**20),
        cost_estimate=pl.CostEstimate(
            flops=slots * 2 * side * side * embed,
            bytes_accessed=2 * (vals.size + (held + total) * side * embed),
            transcendentals=0,
        ),
    )(count, rows, cols, vals, *parts)


def place_requests(owner, local, devices, slots_per):
    hits = (owner[:, None] == jnp.arange(devices, dtype=jnp.int32)[None, :]).astype(jnp.int32)
    rank = jnp.sum((jnp.cumsum(hits, axis=0) - 1) * hits, axis=1)
    slot = owner * slots_per + rank
    request = jnp.zeros((devices * slots_per,), jnp.int32).at[slot].set(local)
    return (slot, request.reshape(devices, slots_per))


def on_device(
    user_emb,
    item_emb,
    tile_vals,
    tile_rows,
    tile_cols,
    tile_count,
    pair_users,
    pair_items,
    negatives,
):
    row_count = lax.axis_size(ROW)
    col_count = lax.axis_size(COL)
    user_dev = user_emb.shape[2]
    item_dev = item_emb.shape[2]
    embed = user_emb.shape[3]
    side = tile_vals.shape[-1]
    user_own = user_emb.reshape(-1, side, embed)
    item_own = item_emb.reshape(-1, side, embed)
    user_each, item_each = user_own.shape[0], item_own.shape[0]
    half = user_each // 2
    slots = (tile_vals[0, 0], tile_rows[0, 0], tile_cols[0, 0], tile_count[0])

    item_tiles, from_x, from_z = first_gather(
        item_own.astype(jnp.bfloat16), user_own.swapaxes(1, 2).astype(jnp.bfloat16)
    )
    spread = [(from_x, 0, 0), (from_z, 0, 1)]
    for step in range(1, SIDE):
        spread.append((shifted(from_x, Z, step), step, 0))
        spread.append((shifted(from_z, X, step), step, 1))

    def user_places(refs):
        for ref, (_, step, late) in zip(refs, spread):
            back = lax.rem(lax.axis_index(X if late else Z) + SIDE - step, SIDE)
            for i in range(SIDE):
                holder = back * SIDE + i if late else i * SIDE + back
                yield ref.at[i], holder * user_each + late * half

    user_part = tile_terms(
        True, *slots, [item_tiles], lambda refs: [(refs[0], 0)],
        item_tiles.shape[0], user_each * col_count,
    )
    item_part = tile_terms(
        False, *slots, [part for part, _, _ in spread], user_places,
        user_each * col_count, item_tiles.shape[0],
    )
    user_final, item_final = settle(user_part, item_part, user_own, item_own)

    devices = row_count * col_count
    slots_per = 2 * pair_users.shape[0] // devices
    user_owner = pair_users // user_dev
    user_local = pair_users % user_dev
    item_holder = pair_items // item_dev
    item_owner = item_holder % row_count * col_count + item_holder // row_count
    item_local = pair_items % item_dev
    user_slot, user_request = place_requests(user_owner, user_local, devices, slots_per)
    item_slot, item_request = place_requests(item_owner, item_local, devices, slots_per)
    requests = jnp.concatenate([user_request, item_request], axis=1)
    wanted = lax.all_to_all(requests, ROW_COL, split_axis=0, concat_axis=0, tiled=True)
    offset = (lax.axis_index(COL) * row_count + lax.axis_index(ROW)) * item_dev
    neg_each = negatives.shape[0] // devices
    device_rank = lax.axis_index(ROW) * col_count + lax.axis_index(COL)
    mine = lax.dynamic_slice_in_dim(negatives, device_rank * neg_each, neg_each, 0) - offset
    user_vec, positive, negative_vec = exchange(
        wanted[:, :slots_per].reshape(-1),
        wanted[:, slots_per:].reshape(-1),
        mine,
        user_final.reshape(-1, embed),
        item_final.reshape(-1, embed),
        user_slot[:, None],
        item_slot[:, None],
    )
    against = jnp.dot(user_vec, negative_vec.T, preferred_element_type=jnp.float32)
    bpr_terms = jnp.log1p(jnp.exp(against - positive))
    return (user_final.reshape(user_emb.shape), item_final.reshape(item_emb.shape), bpr_terms)


def solution(mesh):
    torus = Mesh(mesh.devices.reshape(4, 2, 4, 4), ("row_0", "row_1", "col_0", "col_1"))
    return jax.shard_map(
        on_device,
        mesh=torus,
        in_specs=(
            P(ROW, COL, None, None),
            P(COL, ROW, None, None),
            P(ROW, COL, None, None, None),
            P(ROW, COL, None),
            P(ROW, COL, None),
            P(ROW, COL),
            P(ROW_COL),
            P(ROW_COL),
            P(),
        ),
        out_specs=(P(ROW, COL, None, None), P(COL, ROW, None, None), P(ROW_COL, None)),
        check_vma=False,
    )
```

```python
import functools

import jax
import jax.numpy as jnp
from jax import lax
from jax.experimental import pallas as pl
from jax.experimental.pallas import tpu as pltpu
from jax.sharding import Mesh
from jax.sharding import PartitionSpec as P

ROW = ("row_0", "row_1")
COL = ("col_0", "col_1")
Y, CORE, X, Z = "row_0", "row_1", "col_0", "col_1"
SIDE = 4
ANY = pl.BlockSpec(memory_space=pl.ANY)
VMEM = pl.BlockSpec(memory_space=pltpu.VMEM)
SMEM = pl.BlockSpec(memory_space=pltpu.SMEM)
DMA = pltpu.SemaphoreType.DMA
ROW_COL = ("row_0", "row_1", "col_0", "col_1")


def greet(peers):
    barrier = pltpu.get_barrier_semaphore()
    for peer in peers:
        pl.semaphore_signal(barrier, inc=1, device_id=peer)
    return lambda: pl.semaphore_wait(barrier, len(peers))


def ahead(axis, step):
    return lax.rem(lax.axis_index(axis) + step, SIDE)


def slots_of(pairs, width, turn, devices, each, slot_out):
    count = pairs.shape[1]
    shift = width.bit_length() - 1
    holder = pairs >> shift
    owner = lax.rem(holder, 8) * 16 + holder // 8 if turn else holder
    local = pairs & (width - 1)
    owner_down = jnp.broadcast_to(owner, (128, count)).T[:, :1]
    below = lax.broadcasted_iota(jnp.int32, (count, count), 0)
    right = lax.broadcasted_iota(jnp.int32, (count, count), 1)
    same = owner_down == owner
    before = jnp.where(same & (below < right), 1, 0)
    after = jnp.where(same & (right < below), 1, 0)
    slot = owner * each + jnp.sum(before, axis=0, keepdims=True)
    slot_out[...] = owner_down * each + jnp.sum(after, axis=1, keepdims=True)
    first = lax.broadcasted_iota(jnp.int32, (devices, count), 0) * each
    return [
        jnp.sum(jnp.where(slot == first + k, local, 0), axis=1, keepdims=True) for k in range(each)
    ]


def first_gather_kernel(
    widths, item_emb, user_emb, pair_users, pair_items, items_out, x_out, z_out, user_slot, item_slot, request,
    items, users, table, sent, came, kept,
):
    y, core, x, z = (lax.axis_index(a) for a in (Y, CORE, X, Z))
    shard, half = items.shape[0], users.shape[0] // 2
    other = {CORE: 1 - core}
    steps = range(1, SIDE)
    entered = greet([other] + [{a: ahead(a, s)} for a in (Y, X, Z) for s in steps])
    tile = items.shape[1]
    for i in range(shard):
        items[i] = item_emb[pl.ds(i * tile, tile)].astype(jnp.bfloat16)
    for i in range(2 * half):
        users[i] = user_emb[pl.ds(i * tile, tile)].T.astype(jnp.bfloat16)
    entered()

    def place(y_of, core_of):
        return items_out.at[pl.ds((y_of * 2 + core_of) * shard, shard)]

    def send(k, src, dst, peer):
        copy = pltpu.make_async_remote_copy(src, dst, sent.at[k], came.at[k], device_id=peer)
        copy.start()
        return copy

    copies = []
    to_y = [send(s - 1, items, place(y, core), {Y: ahead(Y, s)}) for s in steps]
    copies.append(send(3, items, place(y, core), other))
    for s in steps:
        copies.append(send(6 + s, users.at[pl.ds(0, half)], x_out.at[x], {X: ahead(X, s)}))
        copies.append(send(9 + s, users.at[pl.ds(half, half)], z_out.at[z], {Z: ahead(Z, s)}))
    local = [
        pltpu.make_async_copy(items, place(y, core), kept.at[0]),
        pltpu.make_async_copy(users.at[pl.ds(0, half)], x_out.at[x], kept.at[1]),
        pltpu.make_async_copy(users.at[pl.ds(half, half)], z_out.at[z], kept.at[2]),
    ]
    for copy in local:
        copy.start()

    devices = request.shape[0]
    each = 2 * pair_users.shape[1] // devices
    wanted = slots_of(pair_users[...], widths[0], False, devices, each, user_slot)
    wanted += slots_of(pair_items[...], widths[1], True, devices, each, item_slot)
    lane = lax.broadcasted_iota(jnp.int32, table.shape, 1)
    spread = jnp.zeros(table.shape, jnp.int32)
    for k, column in enumerate(wanted):
        spread = jnp.where(lane == k, column, spread)
    table[...] = spread

    @pl.loop(0, devices)
    def _(d):
        request[d] = table[pl.ds(d, 1)]

    for s in steps:
        to_y[s - 1].wait()
        back = lax.rem(y + SIDE - s, SIDE)
        copies.append(send(3 + s, place(back, core), place(back, core), other))
    for copy in copies + local:
        copy.wait()


def first_gather(item_emb, user_emb, tile, pair_users, pair_items, widths, devices):
    shard, side = item_emb.shape[0] // tile, (tile, item_emb.shape[1])
    half, count = user_emb.shape[0] // tile // 2, pair_users.shape[1]
    stage = jax.ShapeDtypeStruct((SIDE, half, *side), jnp.bfloat16)
    slot = jax.ShapeDtypeStruct((count, 1), jnp.int32)
    return pl.pallas_call(
        functools.partial(first_gather_kernel, widths),
        name="first_gather",
        out_shape=(
            jax.ShapeDtypeStruct((8 * shard, *side), jnp.bfloat16), stage, stage,
            slot, slot, jax.ShapeDtypeStruct((devices, 1, 128), jnp.int32),
        ),
        in_specs=[VMEM] * 4,
        out_specs=(ANY, ANY, ANY, VMEM, VMEM, VMEM),
        scratch_shapes=[
            pltpu.VMEM((shard, *side), jnp.bfloat16), pltpu.VMEM((2 * half, *side), jnp.bfloat16),
            pltpu.VMEM((devices, 128), jnp.int32), DMA((13,)), DMA((13,)), DMA((3,)),
        ],
        compiler_params=pltpu.CompilerParams(
            collective_id=0, has_side_effects=True, vmem_limit_bytes=58 * 2**20
        ),
    )(item_emb, user_emb, pair_users, pair_items)


def shifted(array, axis, step):
    return lax.ppermute(array, axis, [(i, (i + step) % SIDE) for i in range(SIDE)])


def coords(rank):
    return {Y: rank // 32, CORE: lax.rem(rank // 16, 2), X: lax.rem(rank // 4, 4), Z: lax.rem(rank, 4)}


def settle_kernel(
    devices, each,
    x_own, x_up, x_down, z_own, z_up, z_down, items, user_emb, item_emb, request, user_slot, item_slot, negatives,
    user_out, item_out, margin,
    got_x, got_z, sum_x, sum_z, last_x, last_z, got_i, sum_i, last_i, asked, wanted, stage, packs, arrived,
    sent, came, kept, ready, ask_sent, ask_came, row_sent, row_came,
):
    y, core, x, z = (lax.axis_index(a) for a in (Y, CORE, X, Z))
    me = ((y * 2 + core) * SIDE + x) * SIDE + z
    steps = range(1, SIDE)
    half, tile = got_x.shape[2], got_x.shape[3]
    mates = [{Y: ahead(Y, s), CORE: lax.rem(core + c, 2)} for s in range(SIDE) for c in range(2) if s or c]
    entered = greet([{a: ahead(a, s)} for a in (X, Z) for s in steps] + mates)

    def other(s):
        return lax.rem(me + s, devices)

    def to_others(act, group=8):
        act(list(range(1, group)))

        @pl.loop(1, devices // group)
        def _(g):
            act([g * group + k for k in range(group)])

    loads = [pltpu.make_async_copy(ref, got_x.at[k], kept.at[k]) for k, ref in enumerate((x_own, x_up, x_down))]
    loads += [pltpu.make_async_copy(ref, got_z.at[k], kept.at[4 + k]) for k, ref in enumerate((z_own, z_up, z_down))]
    loads.append(pltpu.make_async_copy(items.at[:, core], got_i.at[0], kept.at[8]))
    for copy in loads:
        copy.start()

    def send(k, src, dst, peer):
        copy = pltpu.make_async_remote_copy(src, dst, sent.at[k], came.at[k], device_id=peer)
        copy.start()
        return copy

    def add_up(parts, to):
        @pl.loop(0, to.shape[0])
        def _(i):
            total = parts[0][i].astype(jnp.float32)
            for part in parts[1:]:
                total += part[i].astype(jnp.float32)
            to[i] = total.astype(to.dtype)

    entered()
    pair = send(0, items.at[:, 1 - core], got_i.at[1], {CORE: 1 - core})
    stages = {
        X: (got_z, 3, sum_z, last_z, 4),
        Z: (got_x, 3, sum_x, last_x, 1),
        Y: (got_i, 2, sum_i, last_i, 7),
    }
    last = {axis: [] for axis in stages}

    def pass_on(axis, s):
        got, parts, total, final, base = stages[axis]
        goal = ahead(axis, s)
        add_up([got.at[j, goal] for j in range(parts)], total.at[s - 1])
        last[axis].append(send(base + s - 1, total.at[s - 1], final.at[s - 1], {axis: goal}))

    for copy in loads[:-1]:
        copy.wait()
    pass_on(Z, 2)
    pass_on(X, 2)
    loads[-1].wait()
    pair.wait()
    for s in (2, 1, 3):
        pass_on(Y, s)
    for s in (1, 3):
        pass_on(Z, s)
        pass_on(X, s)

    for k, axis in enumerate((X, Z)):
        for s in steps:
            pl.semaphore_signal(ready.at[k], inc=1, device_id={axis: ahead(axis, s)})
        pl.semaphore_wait(ready.at[k], 3)

    def ask(group):
        for s in group:
            pltpu.make_async_remote_copy(
                request.at[other(s)], asked.at[me], ask_sent, ask_came, device_id=coords(other(s))
            ).start()

    to_others(ask)
    own_ask = pltpu.make_async_copy(request.at[me], asked.at[me], kept.at[9])
    own_ask.start()
    own_ask.wait()
    rest = pl.ds(0, devices - 1)
    pltpu.make_async_copy(request.at[rest], asked.at[rest], ask_came).wait()
    pltpu.make_async_copy(request.at[rest], asked.at[rest], ask_sent).wait()
    listed = pltpu.make_async_copy(asked, wanted, kept.at[10])
    listed.start()

    def finish(emb, to, start, parts):
        @pl.loop(0, parts[0].shape[0])
        def _(i):
            total = parts[0][i].astype(jnp.float32)
            for part in parts[1:]:
                total += part[i].astype(jnp.float32)
            rows = pl.ds(pl.multiple_of(start + i * tile, tile), tile)
            to[rows] = (emb[rows] + total) * 0.5

    for axis, mine, emb, to, start in (
        (Y, y, item_emb, item_out, 0),
        (Z, z, user_emb, user_out, 0),
        (X, x, user_emb, user_out, half * tile),
    ):
        got, parts, _, final, _ = stages[axis]
        for copy in last[axis]:
            copy.wait()
        finish(emb, to, start, [got.at[j, mine] for j in range(parts)] + [final.at[j] for j in range(3)])
    listed.wait()

    for k in range(each):
        for g in range(stage.shape[0]):
            stage[g, pl.ds(2 * each + k, 1)] = item_out[pl.ds(negatives[k], 1)]

    def pack(goals):
        for g, d in enumerate(goals):
            for k in range(each):
                stage[g, pl.ds(k, 1)] = user_out[pl.ds(wanted[d, 0, k], 1)]
                stage[g, pl.ds(each + k, 1)] = item_out[pl.ds(wanted[d, 0, each + k], 1)]
        for g, d in enumerate(goals):
            packs[d] = stage[g].astype(jnp.bfloat16)

    def give(group):
        goals = [other(s) for s in group]
        pack(goals)
        for d in goals:
            pltpu.make_async_remote_copy(
                packs.at[d], arrived.at[me], row_sent, row_came, device_id=coords(d)
            ).start()

    to_others(give)
    pack([me])
    mine = pltpu.make_async_copy(packs.at[me], arrived.at[me], kept.at[11])
    mine.start()
    mine.wait()
    pltpu.make_async_copy(packs.at[rest], arrived.at[rest], row_came).wait()
    pltpu.make_async_copy(packs.at[rest], arrived.at[rest], row_sent).wait()

    def picked(slot, first):
        rows = arrived[:, pl.ds(first, each)].reshape(devices * each, -1)
        hits = lax.broadcasted_iota(jnp.int32, (slot.shape[0], devices * each), 1) == slot[...]
        return jnp.dot(hits.astype(jnp.bfloat16), rows, preferred_element_type=jnp.float32)

    users = picked(user_slot, 0)
    chosen = picked(item_slot, each)
    positive = jnp.sum(users * chosen, axis=1, keepdims=True)
    against = arrived[:, pl.ds(2 * each, each)].reshape(devices * each, -1)
    margin[...] = (
        lax.dot_general(
            users.astype(jnp.bfloat16), against, (((1,), (1,)), ((), ())),
            preferred_element_type=jnp.float32,
        )
        - positive
    )


def settle(over_x, over_z, items, user_emb, item_emb, request, user_slot, item_slot, negatives):
    side = items.shape[1:]
    embed = user_emb.shape[1]
    half, shard = over_x[0].shape[1], item_emb.shape[0] // side[0]
    items = items.reshape(SIDE, 2, shard, *side)
    devices, each, pairs = request.shape[0], negatives.shape[0], user_slot.shape[0]
    many, one, low = (SIDE, half, *side), (half, *side), jnp.bfloat16
    return pl.pallas_call(
        functools.partial(settle_kernel, devices, each),
        name="settle",
        out_shape=(
            jax.ShapeDtypeStruct(user_emb.shape, jnp.float32),
            jax.ShapeDtypeStruct(item_emb.shape, jnp.float32),
            jax.ShapeDtypeStruct((pairs, devices * each), jnp.float32),
        ),
        in_specs=[ANY] * 7 + [VMEM] * 5 + [SMEM],
        out_specs=(VMEM,) * 3,
        scratch_shapes=[
            pltpu.VMEM((3, *many), low), pltpu.VMEM((3, *many), low),
            pltpu.VMEM((3, *one), low), pltpu.VMEM((3, *one), low),
            pltpu.VMEM((3, *one), low), pltpu.VMEM((3, *one), low),
            pltpu.VMEM((2, SIDE, shard, *side), low), pltpu.VMEM((3, shard, *side), low),
            pltpu.VMEM((3, shard, *side), low),
            pltpu.VMEM((devices, 1, 128), jnp.int32), pltpu.SMEM((devices, 1, 128), jnp.int32),
            pltpu.VMEM((8, 3 * each, embed), jnp.float32),
            pltpu.VMEM((devices, 3 * each, embed), low), pltpu.VMEM((devices, 3 * each, embed), low),
            DMA((10,)), DMA((10,)), DMA((12,)), pltpu.SemaphoreType.REGULAR((2,)), DMA, DMA, DMA, DMA,
        ],
        compiler_params=pltpu.CompilerParams(
            collective_id=1, has_side_effects=True, vmem_limit_bytes=58 * 2**20
        ),
    )(*over_x, *over_z, items, user_emb, item_emb, request, user_slot, item_slot, negatives)


def joined_kernel(*refs):
    for part, came, out in zip(refs[:4], refs[4:8], refs[8:]):
        for i in range(part.shape[1]):
            out[0, i] = (part[0, i].astype(jnp.float32) + came[0, i].astype(jnp.float32)).astype(out.dtype)


def joined(parts, relayed):
    block = (1, *parts[0].shape[1:])
    starts = (0, parts[0].shape[0] // 2) * 2
    spots = [pl.BlockSpec(block, lambda i, start=start: (start + i, 0, 0, 0)) for start in starts]
    return pl.pallas_call(
        joined_kernel,
        name="joined",
        grid=(parts[0].shape[0] // 2,),
        out_shape=[jax.ShapeDtypeStruct(part.shape, part.dtype) for part in parts],
        in_specs=spots + [pl.BlockSpec(block, lambda i: (i, 0, 0, 0))] * 4,
        out_specs=spots,
        input_output_aliases={k: k for k in range(4)},
        compiler_params=pltpu.CompilerParams(vmem_limit_bytes=58 * 2**20),
        cost_estimate=pl.CostEstimate(flops=2**20, bytes_accessed=6 * 2**20, transcendentals=0),
    )(*parts, *relayed)


def tile_kernel(width, depth, users, place, pieces, take, count_ref, rows, cols, vals, *refs):
    parts, outs, (acc, bufs, table, ready, sems, filled, emptied) = refs[:pieces], refs[pieces:-7], refs[-7:]
    total = acc.shape[0] - 1
    count = count_ref[0]
    chunks = (count + width - 1) // width

    def fetch(k, slot):
        return pltpu.make_async_copy(vals.at[pl.ds(k * width, width)], bufs.at[slot], sems.at[slot])

    for k in range(depth - 1):

        @pl.when(k < chunks)
        def _():
            fetch(k, k).start()

    copies = [
        pltpu.make_async_copy(part, table.at[pl.ds(start, part.shape[0])], filled)
        for part, start in place(parts)
    ]
    for copy in copies:
        copy.start()

    @pl.loop(0, total + 1)
    def _(i):
        acc[i] = jnp.zeros(acc.shape[1:], jnp.float32)

    pltpu.make_async_copy(table, table, filled).wait()

    @pl.loop(0, chunks)
    def _(k):
        slot = lax.rem(k, depth)
        ahead = k + depth - 1

        @pl.when(ahead < chunks)
        def _():
            fetch(ahead, lax.rem(ahead, depth)).start()

        fetch(k, slot).wait()
        products = []
        for t in range(width):
            spot = k * width + t
            tile = bufs[slot, t]
            if users:
                left, right, goal = tile, table[cols[spot]], rows[spot]
            else:
                left, right, goal = table[rows[spot]], tile, cols[spot]
            product = jnp.dot(left, right, preferred_element_type=jnp.float32)
            products.append((jnp.where(spot < count, goal, total), product))
        for goal, product in products:
            acc[goal] += product

    for out, start in take(outs):
        rows = pl.ds(start, out.shape[0])

        @pl.loop(0, out.shape[0])
        def _(i, start=start):
            tile = acc[start + i]
            ready[start + i] = (tile if users else tile.T).astype(jnp.bfloat16)

        pltpu.make_async_copy(ready.at[rows], out, emptied).start()
    pltpu.make_async_copy(ready, ready, emptied).wait()


def tile_terms(users, vals, rows, cols, count, parts, place, held, out_shapes, take, width=16, depth=3):
    slots, side, embed = *vals.shape[:2], parts[0].shape[-1]
    total = sum(shape[0] * (shape[1] if len(shape) == 4 else 1) for shape in out_shapes)
    return pl.pallas_call(
        functools.partial(tile_kernel, width, depth, users, place, len(parts), take),
        name="user_terms" if users else "item_terms",
        out_shape=[jax.ShapeDtypeStruct(shape, jnp.bfloat16) for shape in out_shapes],
        in_specs=[SMEM, SMEM, SMEM, ANY] + [ANY] * len(parts),
        out_specs=[ANY] * len(out_shapes),
        scratch_shapes=[
            pltpu.VMEM((total + 1, side, embed), jnp.float32),
            pltpu.VMEM((depth, width, side, side), jnp.bfloat16),
            pltpu.VMEM((held, side, embed), jnp.bfloat16),
            pltpu.VMEM((total, side, embed), jnp.bfloat16),
            DMA((depth,)),
            DMA,
            DMA,
        ],
        compiler_params=pltpu.CompilerParams(vmem_limit_bytes=56 * 2**20),
        cost_estimate=pl.CostEstimate(
            flops=slots * 2 * side * side * embed,
            bytes_accessed=2 * (vals.size + (held + total) * side * embed),
            transcendentals=0,
        ),
    )(count, rows, cols, vals, *parts)


def on_device(
    user_emb,
    item_emb,
    tile_vals,
    tile_rows,
    tile_cols,
    tile_count,
    pair_users,
    pair_items,
    negatives,
):
    row_count = lax.axis_size(ROW)
    col_count = lax.axis_size(COL)
    user_dev = user_emb.shape[2]
    item_dev = item_emb.shape[2]
    embed = user_emb.shape[3]
    side = tile_vals.shape[-1]
    user_each = user_dev // side
    half = user_each // 2
    slots = (tile_vals[0, 0], tile_rows[0, 0], tile_cols[0, 0], tile_count[0])

    devices = row_count * col_count
    neg_each = negatives.shape[0] // devices
    user_rows, item_rows = user_emb.reshape(-1, embed), item_emb.reshape(-1, embed)
    item_tiles, from_x, from_z, user_slot, item_slot, request = first_gather(
        item_rows, user_rows, side, pair_users[None], pair_items[None], (user_dev, item_dev), devices
    )
    near = [(shifted(array, axis, step), 1 if step == 1 else 3, late, 0)
            for step in (1, -1) for array, axis, late in ((from_x, Z, 0), (from_z, X, 1))]

    def item_places(refs):
        return [(refs[0], 0)]

    def item_takes(refs):
        for start in range(0, item_tiles.shape[0], 16):
            yield refs[0].at[pl.ds(start, 16)], start

    def dealt(refs):
        for late, axis in ((0, X), (1, Z)):
            own, up, down, low, high = refs[5 * late : 5 * late + 5]
            for step, to in ((0, own), (1, up), (3, down), (2, None)):
                goal = ahead(axis, step)
                for i in range(SIDE):
                    holder = i * SIDE + goal if late else goal * SIDE + i
                    ref = (low if i < 2 else high).at[i % 2] if to is None else to.at[i]
                    yield ref, holder * user_each + late * half

    many, few = (SIDE, half, side, embed), (SIDE // 2, half, side, embed)
    user_parts = tile_terms(
        True, *slots, [item_tiles], item_places, item_tiles.shape[0],
        [many, many, many, few, few] * 2, dealt,
    )
    relay = []
    for late, axis in ((0, X), (1, Z)):
        for k, step in ((3, 1), (4, -1)):
            relay.append(shifted(user_parts[5 * late + k], axis, step))
    far = []
    for array, back, late, _ in near:
        cut = slice(0, SIDE // 2) if back == 1 else slice(SIDE // 2, SIDE)
        sent_on = shifted(array[cut], X if late else Z, 1 if back == 1 else -1)
        far.append((sent_on, 2, late, cut.start))
    onward = joined([user_parts[k] for k in (1, 2, 6, 7)], relay)
    over_x, over_z = [user_parts[0]], [user_parts[5]]
    for k, (over, axis, step) in enumerate(((over_x, X, 1), (over_x, X, -1), (over_z, Z, 1), (over_z, Z, -1))):
        over.append(shifted(onward[k], axis, step))
    spread = [(from_x, 0, 0, 0), (from_z, 0, 1, 0)] + near + far

    def user_places(refs):
        for ref, (array, back, late, start) in zip(refs, spread):
            at = lax.rem(lax.axis_index(X if late else Z) + SIDE - back, SIDE)
            for i in range(array.shape[0]):
                holder = at * SIDE + start + i if late else (start + i) * SIDE + at
                yield ref.at[i], holder * user_each + late * half

    (item_part,) = tile_terms(
        False, *slots, [part[0] for part in spread], user_places, user_each * col_count,
        [item_tiles.shape], item_takes,
    )
    offset = (lax.axis_index(COL) * row_count + lax.axis_index(ROW)) * item_dev
    device_rank = lax.axis_index(ROW) * col_count + lax.axis_index(COL)
    mine = lax.dynamic_slice_in_dim(negatives, device_rank * neg_each, neg_each, 0) - offset
    user_final, item_final, margin = settle(
        over_x, over_z, item_part, user_rows, item_rows,
        request, user_slot, item_slot, mine,
    )
    bpr_terms = jnp.log1p(jnp.exp(margin))
    return (user_final.reshape(user_emb.shape), item_final.reshape(item_emb.shape), bpr_terms)


def solution(mesh):
    torus = Mesh(mesh.devices.reshape(4, 2, 4, 4), ("row_0", "row_1", "col_0", "col_1"))

    return jax.shard_map(
        on_device,
        mesh=torus,
        in_specs=(
            P(ROW, COL, None, None),
            P(COL, ROW, None, None),
            P(ROW, COL, None, None, None),
            P(ROW, COL, None),
            P(ROW, COL, None),
            P(ROW, COL),
            P(ROW_COL),
            P(ROW_COL),
            P(),
        ),
        out_specs=(P(ROW, COL, None, None), P(COL, ROW, None, None), P(ROW_COL, None)),
        check_vma=False,
    )
```

```python
import functools

import jax
import jax.numpy as jnp
from jax import lax
from jax.experimental import pallas as pl
from jax.experimental.pallas import tpu as pltpu
from jax.sharding import Mesh
from jax.sharding import PartitionSpec as P

ROW = ("row_0", "row_1")
COL = ("col_0", "col_1")
Y, CORE, X, Z = "row_0", "row_1", "col_0", "col_1"
SIDE = 4
ANY = pl.BlockSpec(memory_space=pl.ANY)
VMEM = pl.BlockSpec(memory_space=pltpu.VMEM)
SMEM = pl.BlockSpec(memory_space=pltpu.SMEM)
DMA = pltpu.SemaphoreType.DMA
ROW_COL = ("row_0", "row_1", "col_0", "col_1")


def greet(peers):
    barrier = pltpu.get_barrier_semaphore()
    for peer in peers:
        pl.semaphore_signal(barrier, inc=1, device_id=peer)
    return lambda: pl.semaphore_wait(barrier, len(peers))


def ahead(axis, step):
    return lax.rem(lax.axis_index(axis) + step, SIDE)


def slots_of(pairs, width, turn, devices, each, slot_out):
    count = pairs.shape[1]
    shift = width.bit_length() - 1
    holder = pairs >> shift
    owner = lax.rem(holder, 8) * 16 + holder // 8 if turn else holder
    local = pairs & (width - 1)
    owner_down = jnp.broadcast_to(owner, (128, count)).T[:, :1]
    below = lax.broadcasted_iota(jnp.int32, (count, count), 0)
    right = lax.broadcasted_iota(jnp.int32, (count, count), 1)
    same = owner_down == owner
    before = jnp.where(same & (below < right), 1, 0)
    after = jnp.where(same & (right < below), 1, 0)
    slot = owner * each + jnp.sum(before, axis=0, keepdims=True)
    slot_out[...] = owner_down * each + jnp.sum(after, axis=1, keepdims=True)
    first = lax.broadcasted_iota(jnp.int32, (devices, count), 0) * each
    return [
        jnp.sum(jnp.where(slot == first + k, local, 0), axis=1, keepdims=True) for k in range(each)
    ]


def first_gather_kernel(
    widths, item_emb, user_emb, pair_users, pair_items, items_out, x_out, z_out, user_slot, item_slot, request,
    items, users, table, sent, came, kept,
):
    y, core, x, z = (lax.axis_index(a) for a in (Y, CORE, X, Z))
    shard, half = items.shape[0], users.shape[0] // 2
    other = {CORE: 1 - core}
    steps = range(1, SIDE)
    entered = greet([other] + [{a: ahead(a, s)} for a in (Y, X, Z) for s in steps])
    tile = items.shape[1]
    for i in range(shard):
        items[i] = item_emb[pl.ds(i * tile, tile)].astype(jnp.bfloat16)
    for i in range(2 * half):
        users[i] = user_emb[pl.ds(i * tile, tile)].T.astype(jnp.bfloat16)
    entered()

    def place(y_of, core_of):
        return items_out.at[pl.ds((y_of * 2 + core_of) * shard, shard)]

    def send(k, src, dst, peer):
        copy = pltpu.make_async_remote_copy(src, dst, sent.at[k], came.at[k], device_id=peer)
        copy.start()
        return copy

    ways = {
        Y: (items, lambda i: place(i, core), 0),
        X: (users.at[pl.ds(0, half)], lambda i: x_out.at[i], 4),
        Z: (users.at[pl.ds(half, half)], lambda i: z_out.at[i], 8),
    }
    near = {}
    for axis, (src, spot, base) in ways.items():
        mine = spot(lax.axis_index(axis))
        near[axis] = [send(base + k, src, mine, {axis: ahead(axis, s)}) for k, s in enumerate((1, 3))]
    copies = [send(12, items, place(y, core), other)]
    local = [
        pltpu.make_async_copy(items, place(y, core), kept.at[0]),
        pltpu.make_async_copy(users.at[pl.ds(0, half)], x_out.at[x], kept.at[1]),
        pltpu.make_async_copy(users.at[pl.ds(half, half)], z_out.at[z], kept.at[2]),
    ]
    for copy in local:
        copy.start()

    devices = request.shape[0]
    each = 2 * pair_users.shape[1] // devices
    wanted = slots_of(pair_users[...], widths[0], False, devices, each, user_slot)
    wanted += slots_of(pair_items[...], widths[1], True, devices, each, item_slot)
    lane = lax.broadcasted_iota(jnp.int32, table.shape, 1)
    spread = jnp.zeros(table.shape, jnp.int32)
    for k, column in enumerate(wanted):
        spread = jnp.where(lane == k, column, spread)
    table[...] = spread

    @pl.loop(0, devices)
    def _(d):
        request[d] = table[pl.ds(d, 1)]

    far = []
    for axis, (_, spot, base) in ways.items():
        for k, s in enumerate((1, 3)):
            near[axis][k].wait()
            came_in = spot(ahead(axis, SIDE - s))
            part = came_in.shape[0] // 2
            part = came_in.at[pl.ds(k * part, part)]
            far.append(send(base + 2 + k, part, part, {axis: ahead(axis, s)}))
            if axis == Y:
                copies.append(send(13 + k, came_in, came_in, other))
    for k in range(2):
        far[k].wait()
        part = place(ahead(Y, 2), core).at[pl.ds(k * (shard // 2), shard // 2)]
        copies.append(send(15 + k, part, part, other))
    copies += far[2:]
    for copy in copies + local:
        copy.wait()


def first_gather(item_emb, user_emb, tile, pair_users, pair_items, widths, devices):
    shard, side = item_emb.shape[0] // tile, (tile, item_emb.shape[1])
    half, count = user_emb.shape[0] // tile // 2, pair_users.shape[1]
    stage = jax.ShapeDtypeStruct((SIDE, half, *side), jnp.bfloat16)
    slot = jax.ShapeDtypeStruct((count, 1), jnp.int32)
    return pl.pallas_call(
        functools.partial(first_gather_kernel, widths),
        name="first_gather",
        out_shape=(
            jax.ShapeDtypeStruct((8 * shard, *side), jnp.bfloat16), stage, stage,
            slot, slot, jax.ShapeDtypeStruct((devices, 1, 128), jnp.int32),
        ),
        in_specs=[VMEM] * 4,
        out_specs=(ANY, ANY, ANY, VMEM, VMEM, VMEM),
        scratch_shapes=[
            pltpu.VMEM((shard, *side), jnp.bfloat16), pltpu.VMEM((2 * half, *side), jnp.bfloat16),
            pltpu.VMEM((devices, 128), jnp.int32), DMA((17,)), DMA((17,)), DMA((3,)),
        ],
        compiler_params=pltpu.CompilerParams(
            collective_id=0, has_side_effects=True, vmem_limit_bytes=58 * 2**20
        ),
    )(item_emb, user_emb, pair_users, pair_items)


def shifted(array, axis, step):
    return lax.ppermute(array, axis, [(i, (i + step) % SIDE) for i in range(SIDE)])


def coords(rank):
    return {Y: rank // 32, CORE: lax.rem(rank // 16, 2), X: lax.rem(rank // 4, 4), Z: lax.rem(rank, 4)}


def settle_kernel(
    devices, each,
    x_own, x_up, x_down, z_own, z_up, z_down, items, user_emb, item_emb, request, user_slot, item_slot, negatives,
    user_out, item_out, margin,
    got_x, got_z, sum_x, sum_z, last_x, last_z, got_i, sum_i, last_i, asked, wanted, stage, packs, arrived, chosen_negs,
    sent, came, kept, ready, ask_sent, ask_came, row_sent, row_came,
):
    y, core, x, z = (lax.axis_index(a) for a in (Y, CORE, X, Z))
    me = ((y * 2 + core) * SIDE + x) * SIDE + z
    steps = range(1, SIDE)
    half, tile = got_x.shape[2], got_x.shape[3]
    mates = [{Y: ahead(Y, s), CORE: lax.rem(core + c, 2)} for s in range(SIDE) for c in range(2) if s or c]
    entered = greet([{a: ahead(a, s)} for a in (X, Z) for s in steps] + mates)

    def other(s):
        return lax.rem(me + s, devices)

    def to_others(act, group=8):
        act(list(range(1, group)))

        @pl.loop(1, devices // group)
        def _(g):
            act([g * group + k for k in range(group)])

    loads = [pltpu.make_async_copy(ref, got_x.at[k], kept.at[k]) for k, ref in enumerate((x_own, x_up, x_down))]
    loads += [pltpu.make_async_copy(ref, got_z.at[k], kept.at[4 + k]) for k, ref in enumerate((z_own, z_up, z_down))]
    loads.append(pltpu.make_async_copy(items.at[:, core], got_i.at[0], kept.at[8]))
    for copy in loads:
        copy.start()

    def send(k, src, dst, peer):
        copy = pltpu.make_async_remote_copy(src, dst, sent.at[k], came.at[k], device_id=peer)
        copy.start()
        return copy

    def add_up(parts, to):
        @pl.loop(0, to.shape[0])
        def _(i):
            total = parts[0][i].astype(jnp.float32)
            for part in parts[1:]:
                total += part[i].astype(jnp.float32)
            to[i] = total.astype(to.dtype)

    entered()
    pair = {}
    for s in (2, 1, 3, 0):
        goal = ahead(Y, s)
        pair[s] = send(23 + s, items.at[goal, 1 - core], got_i.at[1, goal], {CORE: 1 - core})
    stages = {
        X: (got_z, 3, sum_z, last_z, 4),
        Z: (got_x, 3, sum_x, last_x, 1),
        Y: (got_i, 2, sum_i, last_i, 7),
    }
    last = {axis: [] for axis in stages}

    def pass_on(axis, s):
        got, parts, total, final, base = stages[axis]
        goal = ahead(axis, s)
        add_up([got.at[j, goal] for j in range(parts)], total.at[s - 1])
        last[axis].append(send(base + s - 1, total.at[s - 1], final.at[s - 1], {axis: goal}))

    for copy in loads[:-1]:
        copy.wait()
    for s in (2, 1, 3):
        pass_on(Z, s)
        pass_on(X, s)
        if s == 2:
            loads[-1].wait()
        pair[s].wait()
        pass_on(Y, s)
    pair[0].wait()

    for k, axis in enumerate((X, Z)):
        for s in steps:
            pl.semaphore_signal(ready.at[k], inc=1, device_id={axis: ahead(axis, s)})
        pl.semaphore_wait(ready.at[k], 3)

    def ask(group):
        for s in group:
            pltpu.make_async_remote_copy(
                request.at[other(s)], asked.at[me], ask_sent, ask_came, device_id=coords(other(s))
            ).start()

    to_others(ask)
    own_ask = pltpu.make_async_copy(request.at[me], asked.at[me], kept.at[9])
    own_ask.start()
    own_ask.wait()
    rest = pl.ds(0, devices - 1)
    pltpu.make_async_copy(request.at[rest], asked.at[rest], ask_came).wait()
    pltpu.make_async_copy(request.at[rest], asked.at[rest], ask_sent).wait()
    listed = pltpu.make_async_copy(asked, wanted, kept.at[10])
    listed.start()

    def finish(emb, to, start, parts):
        @pl.loop(0, parts[0].shape[0])
        def _(i):
            total = parts[0][i].astype(jnp.float32)
            for part in parts[1:]:
                total += part[i].astype(jnp.float32)
            rows = pl.ds(pl.multiple_of(start + i * tile, tile), tile)
            to[rows] = (emb[rows] + total) * 0.5

    def settle_axis(axis, mine, emb, to, start):
        got, parts, _, final, _ = stages[axis]
        for copy in last[axis]:
            copy.wait()
        finish(emb, to, start, [got.at[j, mine] for j in range(parts)] + [final.at[j] for j in range(3)])

    settle_axis(Y, y, item_emb, item_out, 0)
    for k in range(each):
        stage[0, pl.ds(k, 1)] = item_out[pl.ds(negatives[k], 1)]
    group = y * 2 + core
    chosen_negs[group, x, z] = stage[0, pl.ds(0, each)].astype(jnp.bfloat16)
    own = chosen_negs.at[group, x, z]
    first = [send(9 + s, own, own, {X: ahead(X, s)}) for s in steps]
    settle_axis(Z, z, user_emb, user_out, 0)
    settle_axis(X, x, user_emb, user_out, half * tile)
    listed.wait()
    for copy in first:
        copy.wait()
    line = chosen_negs.at[group, :, z]
    second = [send(12 + s, line, line, {Z: ahead(Z, s)}) for s in steps]

    def pack(goals):
        for g, d in enumerate(goals):
            for k in range(each):
                stage[g, pl.ds(k, 1)] = user_out[pl.ds(wanted[d, 0, k], 1)]
                stage[g, pl.ds(each + k, 1)] = item_out[pl.ds(wanted[d, 0, each + k], 1)]
        for g, d in enumerate(goals):
            packs[d] = stage[g].astype(jnp.bfloat16)

    def give(group):
        goals = [other(s) for s in group]
        pack(goals)
        for d in goals:
            pltpu.make_async_remote_copy(
                packs.at[d], arrived.at[me], row_sent, row_came, device_id=coords(d)
            ).start()

    to_others(give)
    for copy in second:
        copy.wait()
    plane = chosen_negs.at[group]
    third = [send(16 + k, plane, plane, mate) for k, mate in enumerate(mates)]
    pack([me])
    mine = pltpu.make_async_copy(packs.at[me], arrived.at[me], kept.at[11])
    mine.start()
    mine.wait()
    pltpu.make_async_copy(packs.at[rest], arrived.at[rest], row_came).wait()
    pltpu.make_async_copy(packs.at[rest], arrived.at[rest], row_sent).wait()
    for copy in third:
        copy.wait()

    def picked(slot, first):
        rows = arrived[:, pl.ds(first, each)].reshape(devices * each, -1)
        hits = lax.broadcasted_iota(jnp.int32, (slot.shape[0], devices * each), 1) == slot[...]
        return jnp.dot(hits.astype(jnp.bfloat16), rows, preferred_element_type=jnp.float32)

    users = picked(user_slot, 0)
    chosen = picked(item_slot, each)
    positive = jnp.sum(users * chosen, axis=1, keepdims=True)
    against = chosen_negs[...].reshape(devices * each, -1)
    margin[...] = (
        lax.dot_general(
            users.astype(jnp.bfloat16), against, (((1,), (1,)), ((), ())),
            preferred_element_type=jnp.float32,
        )
        - positive
    )


def settle(over_x, over_z, items, user_emb, item_emb, request, user_slot, item_slot, negatives):
    side = items.shape[1:]
    embed = user_emb.shape[1]
    half, shard = over_x[0].shape[1], item_emb.shape[0] // side[0]
    items = items.reshape(SIDE, 2, shard, *side)
    devices, each, pairs = request.shape[0], negatives.shape[0], user_slot.shape[0]
    many, one, low = (SIDE, half, *side), (half, *side), jnp.bfloat16
    return pl.pallas_call(
        functools.partial(settle_kernel, devices, each),
        name="settle",
        out_shape=(
            jax.ShapeDtypeStruct(user_emb.shape, jnp.float32),
            jax.ShapeDtypeStruct(item_emb.shape, jnp.float32),
            jax.ShapeDtypeStruct((pairs, devices * each), jnp.float32),
        ),
        in_specs=[ANY] * 7 + [VMEM] * 5 + [SMEM],
        out_specs=(VMEM,) * 3,
        scratch_shapes=[
            pltpu.VMEM((3, *many), low), pltpu.VMEM((3, *many), low),
            pltpu.VMEM((3, *one), low), pltpu.VMEM((3, *one), low),
            pltpu.VMEM((3, *one), low), pltpu.VMEM((3, *one), low),
            pltpu.VMEM((2, SIDE, shard, *side), low), pltpu.VMEM((3, shard, *side), low),
            pltpu.VMEM((3, shard, *side), low),
            pltpu.VMEM((devices, 1, 128), jnp.int32), pltpu.SMEM((devices, 1, 128), jnp.int32),
            pltpu.VMEM((8, 2 * each, embed), jnp.float32),
            pltpu.VMEM((devices, 2 * each, embed), low), pltpu.VMEM((devices, 2 * each, embed), low),
            pltpu.VMEM((2 * SIDE, SIDE, SIDE, each, embed), low),
            DMA((27,)), DMA((27,)), DMA((12,)), pltpu.SemaphoreType.REGULAR((2,)), DMA, DMA, DMA, DMA,
        ],
        compiler_params=pltpu.CompilerParams(
            collective_id=1, has_side_effects=True, vmem_limit_bytes=58 * 2**20
        ),
    )(*over_x, *over_z, items, user_emb, item_emb, request, user_slot, item_slot, negatives)


def joined_kernel(*refs):
    for part, came, out in zip(refs[:4], refs[4:8], refs[8:]):
        for i in range(part.shape[1]):
            out[0, i] = (part[0, i].astype(jnp.float32) + came[0, i].astype(jnp.float32)).astype(out.dtype)


def joined(parts, relayed):
    block = (1, *parts[0].shape[1:])
    starts = (0, parts[0].shape[0] // 2) * 2
    spots = [pl.BlockSpec(block, lambda i, start=start: (start + i, 0, 0, 0)) for start in starts]
    return pl.pallas_call(
        joined_kernel,
        name="joined",
        grid=(parts[0].shape[0] // 2,),
        out_shape=[jax.ShapeDtypeStruct(part.shape, part.dtype) for part in parts],
        in_specs=spots + [pl.BlockSpec(block, lambda i: (i, 0, 0, 0))] * 4,
        out_specs=spots,
        input_output_aliases={k: k for k in range(4)},
        compiler_params=pltpu.CompilerParams(vmem_limit_bytes=58 * 2**20),
        cost_estimate=pl.CostEstimate(flops=2**20, bytes_accessed=6 * 2**20, transcendentals=0),
    )(*parts, *relayed)


def tile_kernel(width, depth, users, place, pieces, take, count_ref, rows, cols, vals, *refs):
    parts, outs, (acc, bufs, table, ready, sems, filled, emptied) = refs[:pieces], refs[pieces:-7], refs[-7:]
    total = acc.shape[0] - 1
    count = count_ref[0]
    chunks = (count + width - 1) // width

    def fetch(k, slot):
        return pltpu.make_async_copy(vals.at[pl.ds(k * width, width)], bufs.at[slot], sems.at[slot])

    for k in range(depth - 1):

        @pl.when(k < chunks)
        def _():
            fetch(k, k).start()

    copies = [
        pltpu.make_async_copy(part, table.at[pl.ds(start, part.shape[0])], filled)
        for part, start in place(parts)
    ]
    for copy in copies:
        copy.start()

    @pl.loop(0, total + 1)
    def _(i):
        acc[i] = jnp.zeros(acc.shape[1:], jnp.float32)

    pltpu.make_async_copy(table, table, filled).wait()

    @pl.loop(0, chunks)
    def _(k):
        slot = lax.rem(k, depth)
        ahead = k + depth - 1

        @pl.when(ahead < chunks)
        def _():
            fetch(ahead, lax.rem(ahead, depth)).start()

        fetch(k, slot).wait()
        products = []
        for t in range(width):
            spot = k * width + t
            tile = bufs[slot, t]
            if users:
                left, right, goal = tile, table[cols[spot]], rows[spot]
            else:
                left, right, goal = table[rows[spot]], tile, cols[spot]
            product = jnp.dot(left, right, preferred_element_type=jnp.float32)
            products.append((jnp.where(spot < count, goal, total), product))
        for goal, product in products:
            acc[goal] += product

    for out, start in take(outs):
        rows = pl.ds(start, out.shape[0])

        @pl.loop(0, out.shape[0])
        def _(i, start=start):
            tile = acc[start + i]
            ready[start + i] = (tile if users else tile.T).astype(jnp.bfloat16)

        pltpu.make_async_copy(ready.at[rows], out, emptied).start()
    pltpu.make_async_copy(ready, ready, emptied).wait()


def tile_terms(users, vals, rows, cols, count, parts, place, held, out_shapes, take, width=64, depth=3):
    slots, side, embed = *vals.shape[:2], parts[0].shape[-1]
    total = sum(shape[0] * (shape[1] if len(shape) == 4 else 1) for shape in out_shapes)
    return pl.pallas_call(
        functools.partial(tile_kernel, width, depth, users, place, len(parts), take),
        name="user_terms" if users else "item_terms",
        out_shape=[jax.ShapeDtypeStruct(shape, jnp.bfloat16) for shape in out_shapes],
        in_specs=[SMEM, SMEM, SMEM, ANY] + [ANY] * len(parts),
        out_specs=[ANY] * len(out_shapes),
        scratch_shapes=[
            pltpu.VMEM((total + 1, side, embed), jnp.float32),
            pltpu.VMEM((depth, width, side, side), jnp.bfloat16),
            pltpu.VMEM((held, side, embed), jnp.bfloat16),
            pltpu.VMEM((total, side, embed), jnp.bfloat16),
            DMA((depth,)),
            DMA,
            DMA,
        ],
        compiler_params=pltpu.CompilerParams(vmem_limit_bytes=56 * 2**20),
        cost_estimate=pl.CostEstimate(
            flops=slots * 2 * side * side * embed,
            bytes_accessed=2 * (vals.size + (held + total) * side * embed),
            transcendentals=0,
        ),
    )(count, rows, cols, vals, *parts)


def on_device(
    user_emb,
    item_emb,
    tile_vals,
    tile_rows,
    tile_cols,
    tile_count,
    pair_users,
    pair_items,
    negatives,
):
    row_count = lax.axis_size(ROW)
    col_count = lax.axis_size(COL)
    user_dev = user_emb.shape[2]
    item_dev = item_emb.shape[2]
    embed = user_emb.shape[3]
    side = tile_vals.shape[-1]
    user_each = user_dev // side
    half = user_each // 2
    slots = (tile_vals[0, 0], tile_rows[0, 0], tile_cols[0, 0], tile_count[0])

    devices = row_count * col_count
    neg_each = negatives.shape[0] // devices
    user_rows, item_rows = user_emb.reshape(-1, embed), item_emb.reshape(-1, embed)
    item_tiles, from_x, from_z, user_slot, item_slot, request = first_gather(
        item_rows, user_rows, side, pair_users[None], pair_items[None], (user_dev, item_dev), devices
    )
    near = [(shifted(array, axis, step), 1 if step == 1 else 3, late, 0)
            for step in (1, -1) for array, axis, late in ((from_x, Z, 0), (from_z, X, 1))]

    def item_places(refs):
        return [(refs[0], 0)]

    def item_takes(refs):
        for start in range(0, item_tiles.shape[0], 16):
            yield refs[0].at[pl.ds(start, 16)], start

    def dealt(refs):
        for late, axis in ((0, X), (1, Z)):
            own, up, down, low, high = refs[5 * late : 5 * late + 5]
            for step, to in ((0, own), (1, up), (3, down), (2, None)):
                goal = ahead(axis, step)
                for i in range(SIDE):
                    holder = i * SIDE + goal if late else goal * SIDE + i
                    ref = (low if i < 2 else high).at[i % 2] if to is None else to.at[i]
                    yield ref, holder * user_each + late * half

    many, few = (SIDE, half, side, embed), (SIDE // 2, half, side, embed)
    user_parts = tile_terms(
        True, *slots, [item_tiles], item_places, item_tiles.shape[0],
        [many, many, many, few, few] * 2, dealt,
    )
    relay = []
    for late, axis in ((0, X), (1, Z)):
        for k, step in ((3, 1), (4, -1)):
            relay.append(shifted(user_parts[5 * late + k], axis, step))
    far = []
    for array, back, late, _ in near:
        cut = slice(0, SIDE // 2) if back == 1 else slice(SIDE // 2, SIDE)
        sent_on = shifted(array[cut], X if late else Z, 1 if back == 1 else -1)
        far.append((sent_on, 2, late, cut.start))
    onward = joined([user_parts[k] for k in (1, 2, 6, 7)], relay)
    over_x, over_z = [user_parts[0]], [user_parts[5]]
    for k, (over, axis, step) in enumerate(((over_x, X, 1), (over_x, X, -1), (over_z, Z, 1), (over_z, Z, -1))):
        over.append(shifted(onward[k], axis, step))
    spread = [(from_x, 0, 0, 0), (from_z, 0, 1, 0)] + near + far

    def user_places(refs):
        for ref, (array, back, late, start) in zip(refs, spread):
            at = lax.rem(lax.axis_index(X if late else Z) + SIDE - back, SIDE)
            for i in range(array.shape[0]):
                holder = at * SIDE + start + i if late else (start + i) * SIDE + at
                yield ref.at[i], holder * user_each + late * half

    (item_part,) = tile_terms(
        False, *slots, [part[0] for part in spread], user_places, user_each * col_count,
        [item_tiles.shape], item_takes,
    )
    offset = (lax.axis_index(COL) * row_count + lax.axis_index(ROW)) * item_dev
    device_rank = lax.axis_index(ROW) * col_count + lax.axis_index(COL)
    mine = lax.dynamic_slice_in_dim(negatives, device_rank * neg_each, neg_each, 0) - offset
    user_final, item_final, margin = settle(
        over_x, over_z, item_part, user_rows, item_rows,
        request, user_slot, item_slot, mine,
    )
    bpr_terms = jnp.log1p(jnp.exp(margin))
    return (user_final.reshape(user_emb.shape), item_final.reshape(item_emb.shape), bpr_terms)


def solution(mesh):
    torus = Mesh(mesh.devices.reshape(4, 2, 4, 4), ("row_0", "row_1", "col_0", "col_1"))

    return jax.shard_map(
        on_device,
        mesh=torus,
        in_specs=(
            P(ROW, COL, None, None),
            P(COL, ROW, None, None),
            P(ROW, COL, None, None, None),
            P(ROW, COL, None),
            P(ROW, COL, None),
            P(ROW, COL),
            P(ROW_COL),
            P(ROW_COL),
            P(),
        ),
        out_specs=(P(ROW, COL, None, None), P(COL, ROW, None, None), P(ROW_COL, None)),
        check_vma=False,
    )
```

```python
import functools

import jax
import jax.numpy as jnp
from jax import lax
from jax.experimental import pallas as pl
from jax.experimental.pallas import tpu as pltpu
from jax.sharding import Mesh
from jax.sharding import PartitionSpec as P

ROW = ("row_0", "row_1")
COL = ("col_0", "col_1")
Y, CORE, X, Z = "row_0", "row_1", "col_0", "col_1"
SIDE = 4
ANY = pl.BlockSpec(memory_space=pl.ANY)
VMEM = pl.BlockSpec(memory_space=pltpu.VMEM)
SMEM = pl.BlockSpec(memory_space=pltpu.SMEM)
DMA = pltpu.SemaphoreType.DMA
WHOLE = 67_043_328
ROW_COL = ("row_0", "row_1", "col_0", "col_1")


def greet(peers):
    barrier = pltpu.get_barrier_semaphore()
    for peer in peers:
        pl.semaphore_signal(barrier, inc=1, device_id=peer)
    return lambda: pl.semaphore_wait(barrier, len(peers))


def ahead(axis, step):
    return lax.rem(lax.axis_index(axis) + step, SIDE)


def slots_of(pairs, width, turn, devices, each, slot_out):
    count = pairs.shape[1]
    shift = width.bit_length() - 1
    holder = pairs >> shift
    owner = lax.rem(holder, 8) * 16 + holder // 8 if turn else holder
    local = pairs & (width - 1)
    owner_down = jnp.broadcast_to(owner, (128, count)).T[:, :1]
    below = lax.broadcasted_iota(jnp.int32, (count, count), 0)
    right = lax.broadcasted_iota(jnp.int32, (count, count), 1)
    same = owner_down == owner
    before = jnp.where(same & (below < right), 1, 0)
    after = jnp.where(same & (right < below), 1, 0)
    slot = owner * each + jnp.sum(before, axis=0, keepdims=True)
    slot_out[...] = owner_down * each + jnp.sum(after, axis=1, keepdims=True)
    first = lax.broadcasted_iota(jnp.int32, (devices, count), 0) * each
    return [
        jnp.sum(jnp.where(slot == first + k, local, 0), axis=1, keepdims=True) for k in range(each)
    ]


def first_gather_kernel(
    widths, item_emb, user_emb, pair_users, pair_items, items_out, x_low, x_high, z_low, z_high, user_slot, item_slot, request,
    item_rows, user_rows, items, users, table, sent, came, kept,
):
    y, core, _, _ = (lax.axis_index(a) for a in (Y, CORE, X, Z))
    shard, half = items.shape[0], users.shape[0] // 2
    other = {CORE: 1 - core}
    steps = range(1, SIDE)
    tile = items.shape[1]
    cut = [pl.ds(k * half * tile, half * tile) for k in range(2)]
    loads = [pltpu.make_async_copy(item_emb, item_rows, kept.at[3])]
    loads += [pltpu.make_async_copy(user_emb.at[c], user_rows.at[c], kept.at[4 + k]) for k, c in enumerate(cut)]
    for copy in loads:
        copy.start()
    entered = greet([other] + [{a: ahead(a, s)} for a in (Y, X, Z) for s in steps])

    def cast_users(k):
        loads[1 + k].wait()
        for i in range(k * half, (k + 1) * half):
            users[i] = user_rows[pl.ds(i * tile, tile)].T.astype(jnp.bfloat16)

    loads[0].wait()
    for i in range(shard):
        items[i] = item_rows[pl.ds(i * tile, tile)].astype(jnp.bfloat16)
    entered()

    def place(y_of, core_of):
        return items_out.at[pl.ds((y_of * 2 + core_of) * shard, shard)]

    def send(k, src, dst, peer):
        copy = pltpu.make_async_remote_copy(src, dst, sent.at[k], came.at[k], device_id=peer)
        copy.start()
        return copy

    ways = {
        Y: (items, lambda i, k: place(i, core).at[pl.ds(k * (shard // 2), shard // 2)]),
        X: (users.at[pl.ds(0, half)], lambda i, k: (x_low, x_high)[k].at[i]),
        Z: (users.at[pl.ds(half, half)], lambda i, k: (z_low, z_high)[k].at[i]),
    }

    def parts_of(axis, i):
        src, spot = ways[axis]
        size = src.shape[0] // 2
        return [(src.at[pl.ds(k * size, size)], spot(i, k)) for k in range(2)]

    near = {}
    for n, axis in enumerate(ways):
        if axis != Y:
            cast_users(0 if axis == X else 1)
        for k, (src, dst) in enumerate(parts_of(axis, lax.axis_index(axis))):
            for j, s in ((k, (1, 3)[k]), (1 - k, (3, 1)[k])):
                near[axis, j, k] = send(4 * n + 2 * j + k, src, dst, {axis: ahead(axis, s)})
    copies = [send(18, items, place(y, core), other)]
    local = [
        pltpu.make_async_copy(items, place(y, core), kept.at[0]),
    ]
    for n, axis in enumerate((X, Z)):
        for k, (src, dst) in enumerate(parts_of(axis, lax.axis_index(axis))):
            local.append(pltpu.make_async_copy(src, dst, kept.at[6 + 2 * n + k]))
    for copy in local:
        copy.start()

    devices = request.shape[0]
    each = 2 * pair_users.shape[1] // devices
    wanted = slots_of(pair_users[...], widths[0], False, devices, each, user_slot)
    wanted += slots_of(pair_items[...], widths[1], True, devices, each, item_slot)
    lane = lax.broadcasted_iota(jnp.int32, table.shape, 1)
    spread = jnp.zeros(table.shape, jnp.int32)
    for k, column in enumerate(wanted):
        spread = jnp.where(lane == k, column, spread)
    table[...] = spread

    @pl.loop(0, devices)
    def _(d):
        request[d] = table[pl.ds(d, 1)]

    far = []
    for n, axis in enumerate(ways):
        for j, s in enumerate((1, 3)):
            back = ahead(axis, SIDE - s)
            near[axis, j, j].wait()
            part = ways[axis][1](back, j)
            far.append(send(12 + 2 * n + j, part, part, {axis: ahead(axis, s)}))
    for j in range(2):
        near[Y, j, 1 - j].wait()
        came_in = place(ahead(Y, SIDE - (1, 3)[j]), core)
        copies.append(send(19 + j, came_in, came_in, other))
    for j in range(2):
        far[j].wait()
        part = ways[Y][1](ahead(Y, 2), j)
        copies.append(send(21 + j, part, part, other))
    copies += [near[axis, j, 1 - j] for axis in (X, Z) for j in range(2)]
    copies += far[2:]
    for copy in copies + local:
        copy.wait()


def first_gather(item_emb, user_emb, tile, pair_users, pair_items, widths, devices):
    shard, side = item_emb.shape[0] // tile, (tile, item_emb.shape[1])
    half, count = user_emb.shape[0] // tile // 2, pair_users.shape[1]
    stage = jax.ShapeDtypeStruct((SIDE, half // 2, *side), jnp.bfloat16)
    slot = jax.ShapeDtypeStruct((count, 1), jnp.int32)
    return pl.pallas_call(
        functools.partial(first_gather_kernel, widths),
        name="first_gather",
        out_shape=(
            jax.ShapeDtypeStruct((8 * shard, *side), jnp.bfloat16), stage, stage, stage, stage,
            slot, slot, jax.ShapeDtypeStruct((devices, 1, 128), jnp.int32),
        ),
        in_specs=[ANY, ANY, VMEM, VMEM],
        out_specs=(ANY,) * 5 + (VMEM,) * 3,
        scratch_shapes=[
            pltpu.VMEM(item_emb.shape, jnp.float32), pltpu.VMEM(user_emb.shape, jnp.float32),
            pltpu.VMEM((shard, *side), jnp.bfloat16), pltpu.VMEM((2 * half, *side), jnp.bfloat16),
            pltpu.VMEM((devices, 128), jnp.int32), DMA((23,)), DMA((23,)), DMA((10,)),
        ],
        compiler_params=pltpu.CompilerParams(
            collective_id=0, has_side_effects=True, vmem_limit_bytes=WHOLE
        ),
    )(item_emb, user_emb, pair_users, pair_items)


def shifted(array, axis, step):
    return lax.ppermute(array, axis, [(i, (i + step) % SIDE) for i in range(SIDE)])


def coords(rank):
    return {Y: rank // 32, CORE: lax.rem(rank // 16, 2), X: lax.rem(rank // 4, 4), Z: lax.rem(rank, 4)}


def settle_kernel(
    devices, each,
    x_own, x_up, x_down, z_own, z_up, z_down, items, user_from, item_from, request, user_slot, item_slot, negatives,
    user_to, item_to, user_vec, positive, negative_vec, user_emb, item_emb, user_out, item_out,
    got_x, got_z, sum_x, sum_z, last_x, last_z, got_i, sum_i, last_i, asked, wanted, stage, packs, arrived, chosen_negs,
    sent, came, kept, ready, ask_sent, ask_came, row_sent, row_came,
):
    y, core, x, z = (lax.axis_index(a) for a in (Y, CORE, X, Z))
    me = ((y * 2 + core) * SIDE + x) * SIDE + z
    steps = range(1, SIDE)
    half, tile = got_x.shape[2], got_x.shape[3]
    mates = [{Y: ahead(Y, s), CORE: lax.rem(core + c, 2)} for s in range(SIDE) for c in range(2) if s or c]
    entered = greet([{a: ahead(a, s)} for a in (X, Z) for s in steps] + mates)

    def other(s):
        return lax.rem(me + s, devices)

    def to_others(act, group=8):
        act(list(range(1, group)))

        @pl.loop(1, devices // group)
        def _(g):
            act([g * group + k for k in range(group)])

    loads = [pltpu.make_async_copy(ref, got_x.at[k], kept.at[k]) for k, ref in enumerate((x_own, x_up, x_down))]
    loads += [pltpu.make_async_copy(ref, got_z.at[k], kept.at[4 + k]) for k, ref in enumerate((z_own, z_up, z_down))]
    loads.append(pltpu.make_async_copy(items.at[:, core], got_i.at[0], kept.at[8]))
    embs = [
        pltpu.make_async_copy(user_from, user_emb, kept.at[3]),
        pltpu.make_async_copy(item_from, item_emb, kept.at[7]),
    ]
    for copy in loads + embs:
        copy.start()

    def send(k, src, dst, peer):
        copy = pltpu.make_async_remote_copy(src, dst, sent.at[k], came.at[k], device_id=peer)
        copy.start()
        return copy

    def add_up(parts, to):
        @pl.loop(0, to.shape[0])
        def _(i):
            total = parts[0][i].astype(jnp.float32)
            for part in parts[1:]:
                total += part[i].astype(jnp.float32)
            to[i] = total.astype(to.dtype)

    entered()
    pair = {}
    for s in (2, 1, 3, 0):
        goal = ahead(Y, s)
        pair[s] = send(23 + s, items.at[goal, 1 - core], got_i.at[1, goal], {CORE: 1 - core})
    stages = {
        X: (got_z, 3, sum_z, last_z, 4),
        Z: (got_x, 3, sum_x, last_x, 1),
        Y: (got_i, 2, sum_i, last_i, 7),
    }
    last = {axis: [] for axis in stages}

    def pass_on(axis, s):
        got, parts, total, final, base = stages[axis]
        goal = ahead(axis, s)
        add_up([got.at[j, goal] for j in range(parts)], total.at[s - 1])
        last[axis].append(send(base + s - 1, total.at[s - 1], final.at[s - 1], {axis: goal}))

    for copy in loads[:-1]:
        copy.wait()
    for s in (2, 1, 3):
        pass_on(Z, s)
        pass_on(X, s)
        if s == 2:
            loads[-1].wait()
        pair[s].wait()
        pass_on(Y, s)
    pair[0].wait()

    for k, axis in enumerate((X, Z)):
        for s in steps:
            pl.semaphore_signal(ready.at[k], inc=1, device_id={axis: ahead(axis, s)})
        pl.semaphore_wait(ready.at[k], 3)

    def ask(group):
        for s in group:
            pltpu.make_async_remote_copy(
                request.at[other(s)], asked.at[me], ask_sent, ask_came, device_id=coords(other(s))
            ).start()

    to_others(ask)
    own_ask = pltpu.make_async_copy(request.at[me], asked.at[me], kept.at[9])
    own_ask.start()
    own_ask.wait()
    rest = pl.ds(0, devices - 1)
    pltpu.make_async_copy(request.at[rest], asked.at[rest], ask_came).wait()
    pltpu.make_async_copy(request.at[rest], asked.at[rest], ask_sent).wait()
    listed = pltpu.make_async_copy(asked, wanted, kept.at[10])
    listed.start()

    def finish(emb, to, start, parts):
        @pl.loop(0, parts[0].shape[0])
        def _(i):
            total = parts[0][i].astype(jnp.float32)
            for part in parts[1:]:
                total += part[i].astype(jnp.float32)
            rows = pl.ds(pl.multiple_of(start + i * tile, tile), tile)
            to[rows] = (emb[rows] + total) * 0.5

    def settle_axis(axis, mine, emb, to, start):
        got, parts, _, final, _ = stages[axis]
        for copy in last[axis]:
            copy.wait()
        finish(emb, to, start, [got.at[j, mine] for j in range(parts)] + [final.at[j] for j in range(3)])

    group = y * 2 + core
    for copy in embs:
        copy.wait()
    settle_axis(Y, y, item_emb, item_out, 0)
    for k in range(each):
        local = lax.rem(negatives[me * each + k], item_out.shape[0])
        stage[0, pl.ds(k, 1)] = item_out[pl.ds(local, 1)]
    chosen_negs[group, x, z] = stage[0, pl.ds(0, each)].astype(jnp.bfloat16)
    own = chosen_negs.at[group, x, z]
    first = [send(9 + s, own, own, {X: ahead(X, s)}) for s in steps]
    settle_axis(Z, z, user_emb, user_out, 0)
    settle_axis(X, x, user_emb, user_out, half * tile)
    stores = [
        pltpu.make_async_copy(user_out, user_to, kept.at[12]),
        pltpu.make_async_copy(item_out, item_to, kept.at[13]),
    ]
    for copy in stores:
        copy.start()
    listed.wait()
    for copy in first:
        copy.wait()
    line = chosen_negs.at[group, :, z]
    second = [send(12 + s, line, line, {Z: ahead(Z, s)}) for s in steps]

    def pack(goals):
        for g, d in enumerate(goals):
            for k in range(each):
                stage[g, pl.ds(k, 1)] = user_out[pl.ds(wanted[d, 0, k], 1)]
                stage[g, pl.ds(each + k, 1)] = item_out[pl.ds(wanted[d, 0, each + k], 1)]
        for g, d in enumerate(goals):
            packs[d] = stage[g].astype(jnp.bfloat16)

    def give(group):
        goals = [other(s) for s in group]
        pack(goals)
        for d in goals:
            pltpu.make_async_remote_copy(
                packs.at[d], arrived.at[me], row_sent, row_came, device_id=coords(d)
            ).start()

    to_others(give)
    for copy in second:
        copy.wait()
    plane = chosen_negs.at[group]
    third = [send(16 + k, plane, plane, mate) for k, mate in enumerate(mates)]
    pack([me])
    mine = pltpu.make_async_copy(packs.at[me], arrived.at[me], kept.at[11])
    mine.start()
    mine.wait()
    pltpu.make_async_copy(packs.at[rest], arrived.at[rest], row_came).wait()
    pltpu.make_async_copy(packs.at[rest], arrived.at[rest], row_sent).wait()
    for copy in third:
        copy.wait()

    def picked(slot, first):
        rows = arrived[:, pl.ds(first, each)].reshape(devices * each, -1)
        hits = lax.broadcasted_iota(jnp.int32, (slot.shape[0], devices * each), 1) == slot[...]
        return jnp.dot(hits.astype(jnp.bfloat16), rows, preferred_element_type=jnp.float32)

    users = picked(user_slot, 0)
    chosen = picked(item_slot, each)
    positive[...] = jnp.sum(users * chosen, axis=1, keepdims=True)
    user_vec[...] = users.astype(jnp.bfloat16)
    negative_vec[...] = chosen_negs[...].reshape(devices * each, -1)
    for copy in stores:
        copy.wait()


def settle(over_x, over_z, items, user_emb, item_emb, request, user_slot, item_slot, negatives):
    side = items.shape[1:]
    embed = user_emb.shape[1]
    half, shard = over_x[0].shape[1], item_emb.shape[0] // side[0]
    items = items.reshape(SIDE, 2, shard, *side)
    devices, pairs = request.shape[0], user_slot.shape[0]
    each = negatives.shape[0] // devices
    many, one, low = (SIDE, half, *side), (half, *side), jnp.bfloat16
    return pl.pallas_call(
        functools.partial(settle_kernel, devices, each),
        name="settle",
        out_shape=(
            jax.ShapeDtypeStruct(user_emb.shape, jnp.float32),
            jax.ShapeDtypeStruct(item_emb.shape, jnp.float32),
            jax.ShapeDtypeStruct((pairs, embed), low),
            jax.ShapeDtypeStruct((pairs, 1), jnp.float32),
            jax.ShapeDtypeStruct((devices * each, embed), low),
        ),
        in_specs=[ANY] * 9 + [VMEM] * 3 + [SMEM],
        out_specs=(ANY, ANY, VMEM, VMEM, VMEM),
        scratch_shapes=[
            pltpu.VMEM(user_emb.shape, jnp.float32), pltpu.VMEM(item_emb.shape, jnp.float32),
            pltpu.VMEM(user_emb.shape, jnp.float32), pltpu.VMEM(item_emb.shape, jnp.float32),
            pltpu.VMEM((3, *many), low), pltpu.VMEM((3, *many), low),
            pltpu.VMEM((3, *one), low), pltpu.VMEM((3, *one), low),
            pltpu.VMEM((3, *one), low), pltpu.VMEM((3, *one), low),
            pltpu.VMEM((2, SIDE, shard, *side), low), pltpu.VMEM((3, shard, *side), low),
            pltpu.VMEM((3, shard, *side), low),
            pltpu.VMEM((devices, 1, 128), jnp.int32), pltpu.SMEM((devices, 1, 128), jnp.int32),
            pltpu.VMEM((8, 2 * each, embed), jnp.float32),
            pltpu.VMEM((devices, 2 * each, embed), low), pltpu.VMEM((devices, 2 * each, embed), low),
            pltpu.VMEM((2 * SIDE, SIDE, SIDE, each, embed), low),
            DMA((27,)), DMA((27,)), DMA((14,)), pltpu.SemaphoreType.REGULAR((2,)), DMA, DMA, DMA, DMA,
        ],
        compiler_params=pltpu.CompilerParams(
            collective_id=1, has_side_effects=True, vmem_limit_bytes=WHOLE
        ),
    )(*over_x, *over_z, items, user_emb, item_emb, request, user_slot, item_slot, negatives)


def last_kernel(user_vec, positive, negative_vec, users, items, terms, users_out, items_out):
    margin = lax.dot_general(
        user_vec[...], negative_vec[...], (((1,), (1,)), ((), ())), preferred_element_type=jnp.float32
    )
    terms[...] = jnp.log1p(jnp.exp(margin - positive[...]))
    users_out[...] = users[...]
    items_out[...] = items[...]


def last(user_vec, positive, negative_vec, users, items, steps=4):
    def block(array):
        return pl.BlockSpec((array.shape[0] // steps, array.shape[1]), lambda i: (i, 0))

    terms = jax.ShapeDtypeStruct((user_vec.shape[0], negative_vec.shape[0]), jnp.float32)
    return pl.pallas_call(
        last_kernel,
        name="last",
        grid=(steps,),
        out_shape=[terms] + [jax.ShapeDtypeStruct(array.shape, array.dtype) for array in (users, items)],
        in_specs=[block(user_vec), block(positive), pl.BlockSpec(negative_vec.shape, lambda i: (0, 0)), block(users), block(items)],
        out_specs=[block(terms), block(users), block(items)],
        compiler_params=pltpu.CompilerParams(vmem_limit_bytes=WHOLE),
    )(user_vec, positive, negative_vec, users, items)


def joined_kernel(*refs):
    for part, came, out in zip(refs[:4], refs[4:8], refs[8:]):
        for i in range(part.shape[1]):
            out[0, i] = (part[0, i].astype(jnp.float32) + came[0, i].astype(jnp.float32)).astype(out.dtype)


def joined(parts, relayed):
    block = (1, *parts[0].shape[1:])
    starts = (0, parts[0].shape[0] // 2) * 2
    spots = [pl.BlockSpec(block, lambda i, start=start: (start + i, 0, 0, 0)) for start in starts]
    return pl.pallas_call(
        joined_kernel,
        name="joined",
        grid=(parts[0].shape[0] // 2,),
        out_shape=[jax.ShapeDtypeStruct(part.shape, part.dtype) for part in parts],
        in_specs=spots + [pl.BlockSpec(block, lambda i: (i, 0, 0, 0))] * 4,
        out_specs=spots,
        input_output_aliases={k: k for k in range(4)},
        compiler_params=pltpu.CompilerParams(vmem_limit_bytes=WHOLE),
        cost_estimate=pl.CostEstimate(flops=2**20, bytes_accessed=6 * 2**20, transcendentals=0),
    )(*parts, *relayed)


def tile_kernel(width, depth, users, place, pieces, take, count_ref, rows, cols, vals, *refs):
    parts, outs, (acc, bufs, table, ready, sems, filled, emptied) = refs[:pieces], refs[pieces:-7], refs[-7:]
    total = acc.shape[0] - 1
    count = count_ref[0]
    chunks = (count + width - 1) // width

    def fetch(k, slot):
        return pltpu.make_async_copy(vals.at[pl.ds(k * width, width)], bufs.at[slot], sems.at[slot])

    for k in range(depth - 1):

        @pl.when(k < chunks)
        def _():
            fetch(k, k).start()

    copies = [
        pltpu.make_async_copy(part, table.at[pl.ds(start, part.shape[0])], filled)
        for part, start in place(parts)
    ]
    for copy in copies:
        copy.start()

    @pl.loop(0, total + 1)
    def _(i):
        acc[i] = jnp.zeros(acc.shape[1:], jnp.float32)

    pltpu.make_async_copy(table, table, filled).wait()

    @pl.loop(0, chunks)
    def _(k):
        slot = lax.rem(k, depth)
        ahead = k + depth - 1

        @pl.when(ahead < chunks)
        def _():
            fetch(ahead, lax.rem(ahead, depth)).start()

        fetch(k, slot).wait()
        products = []
        for t in range(width):
            spot = k * width + t
            tile = bufs[slot, t]
            if users:
                left, right, goal = tile, table[cols[spot]], rows[spot]
            else:
                left, right, goal = table[rows[spot]], tile, cols[spot]
            product = jnp.dot(left, right, preferred_element_type=jnp.float32)
            products.append((jnp.where(spot < count, goal, total), product))
        for goal, product in products:
            acc[goal] += product

    for out, start in take(outs):
        rows = pl.ds(start, out.shape[0])

        @pl.loop(0, out.shape[0])
        def _(i, start=start):
            tile = acc[start + i]
            ready[start + i] = (tile if users else tile.T).astype(jnp.bfloat16)

        pltpu.make_async_copy(ready.at[rows], out, emptied).start()
    pltpu.make_async_copy(ready, ready, emptied).wait()


def tile_terms(users, vals, rows, cols, count, parts, place, held, out_shapes, take, width=64, depth=3):
    slots, side, embed = *vals.shape[:2], parts[0].shape[-1]
    total = sum(shape[0] * (shape[1] if len(shape) == 4 else 1) for shape in out_shapes)
    return pl.pallas_call(
        functools.partial(tile_kernel, width, depth, users, place, len(parts), take),
        name="user_terms" if users else "item_terms",
        out_shape=[jax.ShapeDtypeStruct(shape, jnp.bfloat16) for shape in out_shapes],
        in_specs=[SMEM, SMEM, SMEM, ANY] + [ANY] * len(parts),
        out_specs=[ANY] * len(out_shapes),
        scratch_shapes=[
            pltpu.VMEM((total + 1, side, embed), jnp.float32),
            pltpu.VMEM((depth, width, side, side), jnp.bfloat16),
            pltpu.VMEM((held, side, embed), jnp.bfloat16),
            pltpu.VMEM((total, side, embed), jnp.bfloat16),
            DMA((depth,)),
            DMA,
            DMA,
        ],
        compiler_params=pltpu.CompilerParams(vmem_limit_bytes=WHOLE),
        cost_estimate=pl.CostEstimate(
            flops=slots * 2 * side * side * embed,
            bytes_accessed=2 * (vals.size + (held + total) * side * embed),
            transcendentals=0,
        ),
    )(count, rows, cols, vals, *parts)


def on_device(
    user_emb,
    item_emb,
    tile_vals,
    tile_rows,
    tile_cols,
    tile_count,
    pair_users,
    pair_items,
    negatives,
):
    row_count = lax.axis_size(ROW)
    col_count = lax.axis_size(COL)
    user_dev = user_emb.shape[2]
    item_dev = item_emb.shape[2]
    embed = user_emb.shape[3]
    side = tile_vals.shape[-1]
    user_each = user_dev // side
    half = user_each // 2
    slots = (tile_vals[0, 0], tile_rows[0, 0], tile_cols[0, 0], tile_count[0])

    devices = row_count * col_count
    user_rows, item_rows = user_emb.reshape(-1, embed), item_emb.reshape(-1, embed)
    item_tiles, x_low, x_high, z_low, z_high, user_slot, item_slot, request = first_gather(
        item_rows, user_rows, side, pair_users[None], pair_items[None], (user_dev, item_dev), devices
    )
    held = [(x_low, 0, 0, 0), (x_high, 0, 0, 1), (z_low, 0, 1, 0), (z_high, 0, 1, 1)]
    near = []
    for first in (True, False):
        for array, _, late, k in held:
            step = 1 if (k == 0) == first else -1
            moved = shifted(array, X if late else Z, step)
            near.append((moved, SIDE - 1 if step == -1 else 1, late, k))

    def item_places(refs):
        return [(refs[0], 0)]

    def item_takes(refs):
        for start in range(0, item_tiles.shape[0], 16):
            yield refs[0].at[pl.ds(start, 16)], start

    def dealt(refs):
        for late, axis in ((0, X), (1, Z)):
            own, up, down, low, high = refs[5 * late : 5 * late + 5]
            for step, to in ((0, own), (1, up), (3, down), (2, None)):
                goal = ahead(axis, step)
                for i in range(SIDE):
                    holder = i * SIDE + goal if late else goal * SIDE + i
                    ref = (low if i < 2 else high).at[i % 2] if to is None else to.at[i]
                    yield ref, holder * user_each + late * half

    many, few = (SIDE, half, side, embed), (SIDE // 2, half, side, embed)
    user_parts = tile_terms(
        True, *slots, [item_tiles], item_places, item_tiles.shape[0],
        [many, many, many, few, few] * 2, dealt,
    )
    relay = []
    for late, axis in ((0, X), (1, Z)):
        for k, step in ((3, 1), (4, -1)):
            relay.append(shifted(user_parts[5 * late + k], axis, step))
    far = []
    for array, back, late, k in near[:4]:
        sent_on = shifted(array, X if late else Z, 1 if back == 1 else -1)
        far.append((sent_on, 2, late, k))
    onward = joined([user_parts[k] for k in (1, 2, 6, 7)], relay)
    over_x, over_z = [user_parts[0]], [user_parts[5]]
    for k, (over, axis, step) in enumerate(((over_x, X, 1), (over_x, X, -1), (over_z, Z, 1), (over_z, Z, -1))):
        over.append(shifted(onward[k], axis, step))
    spread = held + near + far

    def user_places(refs):
        for ref, (array, back, late, k) in zip(refs, spread):
            at = lax.rem(lax.axis_index(X if late else Z) + SIDE - back, SIDE)
            for i in range(SIDE):
                holder = at * SIDE + i if late else i * SIDE + at
                yield ref.at[i], holder * user_each + late * half + k * (half // 2)

    (item_part,) = tile_terms(
        False, *slots, [part[0] for part in spread], user_places, user_each * col_count,
        [item_tiles.shape], item_takes,
    )
    user_final, item_final, user_vec, positive, negative_vec = settle(
        over_x, over_z, item_part, user_rows, item_rows, request, user_slot, item_slot, negatives
    )
    bpr_terms, user_final, item_final = last(user_vec, positive, negative_vec, user_final, item_final)
    return (user_final.reshape(user_emb.shape), item_final.reshape(item_emb.shape), bpr_terms)


def solution(mesh):
    torus = Mesh(mesh.devices.reshape(4, 2, 4, 4), ("row_0", "row_1", "col_0", "col_1"))

    return jax.shard_map(
        on_device,
        mesh=torus,
        in_specs=(
            P(ROW, COL, None, None),
            P(COL, ROW, None, None),
            P(ROW, COL, None, None, None),
            P(ROW, COL, None),
            P(ROW, COL, None),
            P(ROW, COL),
            P(ROW_COL),
            P(ROW_COL),
            P(),
        ),
        out_specs=(P(ROW, COL, None, None), P(COL, ROW, None, None), P(ROW_COL, None)),
        check_vma=False,
    )
```

```python
import functools

import jax
import jax.numpy as jnp
from jax import lax
from jax.experimental import pallas as pl
from jax.experimental.pallas import tpu as pltpu
from jax.sharding import Mesh
from jax.sharding import PartitionSpec as P

ROW = ("row_0", "row_1")
COL = ("col_0", "col_1")
Y, CORE, X, Z = "row_0", "row_1", "col_0", "col_1"
SIDE = 4
ANY = pl.BlockSpec(memory_space=pl.ANY)
VMEM = pl.BlockSpec(memory_space=pltpu.VMEM)
SMEM = pl.BlockSpec(memory_space=pltpu.SMEM)
DMA = pltpu.SemaphoreType.DMA
WHOLE = 67_043_328
ROW_COL = ("row_0", "row_1", "col_0", "col_1")


def greet(peers):
    barrier = pltpu.get_barrier_semaphore()
    for peer in peers:
        pl.semaphore_signal(barrier, inc=1, device_id=peer)
    return lambda: pl.semaphore_wait(barrier, len(peers))


def ahead(axis, step):
    return lax.rem(lax.axis_index(axis) + step, SIDE)


def slots_of(pairs, width, turn, devices, each, slot_out):
    count = pairs.shape[1]
    shift = width.bit_length() - 1
    holder = pairs >> shift
    owner = lax.rem(holder, 8) * 16 + holder // 8 if turn else holder
    local = pairs & (width - 1)
    owner_down = jnp.broadcast_to(owner, (128, count)).T[:, :1]
    below = lax.broadcasted_iota(jnp.int32, (count, count), 0)
    right = lax.broadcasted_iota(jnp.int32, (count, count), 1)
    same = owner_down == owner
    before = jnp.where(same & (below < right), 1, 0)
    after = jnp.where(same & (right < below), 1, 0)
    slot = owner * each + jnp.sum(before, axis=0, keepdims=True)
    slot_out[...] = owner_down * each + jnp.sum(after, axis=1, keepdims=True)
    first = lax.broadcasted_iota(jnp.int32, (devices, count), 0) * each
    return [
        jnp.sum(jnp.where(slot == first + k, local, 0), axis=1, keepdims=True) for k in range(each)
    ]


def first_gather_kernel(
    widths, item_emb, user_emb, pair_users, pair_items, items_out, x_low, x_high, z_low, z_high, user_slot, item_slot, request,
    item_rows, user_rows, items, users, table, sent, came, kept,
):
    y, core, _, _ = (lax.axis_index(a) for a in (Y, CORE, X, Z))
    shard, half = items.shape[0], users.shape[0] // 2
    other = {CORE: 1 - core}
    steps = range(1, SIDE)
    tile = items.shape[1]
    cut = [pl.ds(k * half * tile, half * tile) for k in range(2)]
    loads = [pltpu.make_async_copy(item_emb, item_rows, kept.at[3])]
    loads += [pltpu.make_async_copy(user_emb.at[c], user_rows.at[c], kept.at[4 + k]) for k, c in enumerate(cut)]
    for copy in loads:
        copy.start()
    entered = greet([other] + [{a: ahead(a, s)} for a in (Y, X, Z) for s in steps])

    def cast_users(k):
        loads[1 + k].wait()
        for i in range(k * half, (k + 1) * half):
            users[i] = user_rows[pl.ds(i * tile, tile)].T.astype(jnp.bfloat16)

    loads[0].wait()
    for i in range(shard):
        items[i] = item_rows[pl.ds(i * tile, tile)].astype(jnp.bfloat16)
    entered()

    def place(y_of, core_of):
        return items_out.at[pl.ds((y_of * 2 + core_of) * shard, shard)]

    def send(k, src, dst, peer):
        copy = pltpu.make_async_remote_copy(src, dst, sent.at[k], came.at[k], device_id=peer)
        copy.start()
        return copy

    ways = {
        Y: (items, lambda i, k: place(i, core).at[pl.ds(k * (shard // 2), shard // 2)]),
        X: (users.at[pl.ds(0, half)], lambda i, k: (x_low, x_high)[k].at[i]),
        Z: (users.at[pl.ds(half, half)], lambda i, k: (z_low, z_high)[k].at[i]),
    }

    def parts_of(axis, i):
        src, spot = ways[axis]
        size = src.shape[0] // 2
        return [(src.at[pl.ds(k * size, size)], spot(i, k)) for k in range(2)]

    near = {}
    for n, axis in enumerate(ways):
        if axis != Y:
            cast_users(0 if axis == X else 1)
        for k, (src, dst) in enumerate(parts_of(axis, lax.axis_index(axis))):
            for j, s in ((k, (1, 3)[k]), (1 - k, (3, 1)[k])):
                near[axis, j, k] = send(4 * n + 2 * j + k, src, dst, {axis: ahead(axis, s)})
    copies = [send(18, items, place(y, core), other)]
    local = [
        pltpu.make_async_copy(items, place(y, core), kept.at[0]),
    ]
    for n, axis in enumerate((X, Z)):
        for k, (src, dst) in enumerate(parts_of(axis, lax.axis_index(axis))):
            local.append(pltpu.make_async_copy(src, dst, kept.at[6 + 2 * n + k]))
    for copy in local:
        copy.start()

    devices = request.shape[0]
    each = 2 * pair_users.shape[1] // devices
    wanted = slots_of(pair_users[...], widths[0], False, devices, each, user_slot)
    wanted += slots_of(pair_items[...], widths[1], True, devices, each, item_slot)
    lane = lax.broadcasted_iota(jnp.int32, table.shape, 1)
    spread = jnp.zeros(table.shape, jnp.int32)
    for k, column in enumerate(wanted):
        spread = jnp.where(lane == k, column, spread)
    table[...] = spread

    @pl.loop(0, devices)
    def _(d):
        request[d] = table[pl.ds(d, 1)]

    far = []
    for n, axis in enumerate(ways):
        for j, s in enumerate((1, 3)):
            back = ahead(axis, SIDE - s)
            near[axis, j, j].wait()
            part = ways[axis][1](back, j)
            far.append(send(12 + 2 * n + j, part, part, {axis: ahead(axis, s)}))
    for j in range(2):
        near[Y, j, 1 - j].wait()
        came_in = place(ahead(Y, SIDE - (1, 3)[j]), core)
        copies.append(send(19 + j, came_in, came_in, other))
    for j in range(2):
        far[j].wait()
        part = ways[Y][1](ahead(Y, 2), j)
        copies.append(send(21 + j, part, part, other))
    copies += [near[axis, j, 1 - j] for axis in (X, Z) for j in range(2)]
    copies += far[2:]
    for copy in copies + local:
        copy.wait()


def first_gather(item_emb, user_emb, tile, pair_users, pair_items, widths, devices):
    shard, side = item_emb.shape[0] // tile, (tile, item_emb.shape[1])
    half, count = user_emb.shape[0] // tile // 2, pair_users.shape[1]
    stage = jax.ShapeDtypeStruct((SIDE, half // 2, *side), jnp.bfloat16)
    slot = jax.ShapeDtypeStruct((count, 1), jnp.int32)
    return pl.pallas_call(
        functools.partial(first_gather_kernel, widths),
        name="first_gather",
        out_shape=(
            jax.ShapeDtypeStruct((8 * shard, *side), jnp.bfloat16), stage, stage, stage, stage,
            slot, slot, jax.ShapeDtypeStruct((devices, 1, 128), jnp.int32),
        ),
        in_specs=[ANY, ANY, VMEM, VMEM],
        out_specs=(ANY,) * 5 + (VMEM,) * 3,
        scratch_shapes=[
            pltpu.VMEM(item_emb.shape, jnp.float32), pltpu.VMEM(user_emb.shape, jnp.float32),
            pltpu.VMEM((shard, *side), jnp.bfloat16), pltpu.VMEM((2 * half, *side), jnp.bfloat16),
            pltpu.VMEM((devices, 128), jnp.int32), DMA((23,)), DMA((23,)), DMA((10,)),
        ],
        compiler_params=pltpu.CompilerParams(
            collective_id=0, has_side_effects=True, vmem_limit_bytes=WHOLE
        ),
    )(item_emb, user_emb, pair_users, pair_items)


def shifted(array, axis, step):
    return lax.ppermute(array, axis, [(i, (i + step) % SIDE) for i in range(SIDE)])


def coords(rank):
    return {Y: rank // 32, CORE: lax.rem(rank // 16, 2), X: lax.rem(rank // 4, 4), Z: lax.rem(rank, 4)}


def settle_kernel(
    devices, each,
    x_own, x_up, x_down, z_own, z_up, z_down, items, user_from, item_from, request, user_slot, item_slot, negatives,
    user_to, item_to, user_vec, positive, negative_vec, user_emb, item_emb, user_out, item_out,
    got_x, got_z, sum_x, sum_z, last_x, last_z, got_i, sum_i, last_i, asked, wanted, stage, packs, arrived, chosen_negs,
    sent, came, kept, ready, ask_sent, ask_came, row_sent, row_came,
):
    y, core, x, z = (lax.axis_index(a) for a in (Y, CORE, X, Z))
    me = ((y * 2 + core) * SIDE + x) * SIDE + z
    steps = range(1, SIDE)
    half, tile = got_x.shape[2], got_x.shape[3]
    mates = [{Y: ahead(Y, s), CORE: lax.rem(core + c, 2)} for s in range(SIDE) for c in range(2) if s or c]
    entered = greet([{a: ahead(a, s)} for a in (X, Z) for s in steps] + mates)

    def other(s):
        return lax.rem(me + s, devices)

    def to_others(act, group=8):
        count = devices // group - 1

        @pl.loop(0, count)
        def _(h):
            g = lax.rem(h + count // SIDE, count) + 1
            act([g * group + k for k in range(group)])

        act(list(range(1, group)))

    loads = [pltpu.make_async_copy(ref, got_x.at[k], kept.at[k]) for k, ref in enumerate((x_own, x_up, x_down))]
    loads += [pltpu.make_async_copy(ref, got_z.at[k], kept.at[4 + k]) for k, ref in enumerate((z_own, z_up, z_down))]
    loads.append(pltpu.make_async_copy(items.at[:, core], got_i.at[0], kept.at[8]))
    embs = [
        pltpu.make_async_copy(user_from, user_emb, kept.at[3]),
        pltpu.make_async_copy(item_from, item_emb, kept.at[7]),
    ]
    for copy in loads + embs:
        copy.start()

    def send(k, src, dst, peer):
        copy = pltpu.make_async_remote_copy(src, dst, sent.at[k], came.at[k], device_id=peer)
        copy.start()
        return copy

    def add_up(parts, to):
        @pl.loop(0, to.shape[0])
        def _(i):
            total = parts[0][i].astype(jnp.float32)
            for part in parts[1:]:
                total += part[i].astype(jnp.float32)
            to[i] = total.astype(to.dtype)

    stages = {
        X: (got_z, 3, sum_z, last_z, 4),
        Z: (got_x, 3, sum_x, last_x, 1),
        Y: (got_i, 2, sum_i, last_i, 7),
    }
    last = {axis: [] for axis in stages}

    def sum_for(axis, s):
        got, parts, total, _, _ = stages[axis]
        goal = ahead(axis, s)
        add_up([got.at[j, goal] for j in range(parts)], total.at[s - 1])

    def give_sum(axis, s):
        _, _, total, final, base = stages[axis]
        goal = ahead(axis, s)
        last[axis].append(send(base + s - 1, total.at[s - 1], final.at[s - 1], {axis: goal}))

    for copy in loads[:-1]:
        copy.wait()
    for axis in (Z, X):
        sum_for(axis, 2)
    entered()
    pair = {}
    for s in (2, 1, 3, 0):
        goal = ahead(Y, s)
        pair[s] = send(23 + s, items.at[goal, 1 - core], got_i.at[1, goal], {CORE: 1 - core})
    for axis in (Z, X):
        give_sum(axis, 2)
    loads[-1].wait()
    pair[2].wait()
    sum_for(Y, 2)
    give_sum(Y, 2)
    for s in (1, 3):
        for axis in (Z, X, Y):
            if axis == Y:
                pair[s].wait()
            sum_for(axis, s)
            give_sum(axis, s)
    pair[0].wait()

    for k, axis in enumerate((X, Z)):
        for s in steps:
            pl.semaphore_signal(ready.at[k], inc=1, device_id={axis: ahead(axis, s)})
        pl.semaphore_wait(ready.at[k], 3)

    def ask(group):
        for s in group:
            pltpu.make_async_remote_copy(
                request.at[other(s)], asked.at[me], ask_sent, ask_came, device_id=coords(other(s))
            ).start()

    to_others(ask)
    own_ask = pltpu.make_async_copy(request.at[me], asked.at[me], kept.at[9])
    own_ask.start()
    rest = pl.ds(0, devices - 1)

    def finish(emb, to, start, parts):
        @pl.loop(0, parts[0].shape[0])
        def _(i):
            total = parts[0][i].astype(jnp.float32)
            for part in parts[1:]:
                total += part[i].astype(jnp.float32)
            rows = pl.ds(pl.multiple_of(start + i * tile, tile), tile)
            to[rows] = (emb[rows] + total) * 0.5

    def settle_axis(axis, mine, emb, to, start):
        got, parts, _, final, _ = stages[axis]
        for copy in last[axis]:
            copy.wait()
        finish(emb, to, start, [got.at[j, mine] for j in range(parts)] + [final.at[j] for j in range(3)])

    group = y * 2 + core
    for copy in embs:
        copy.wait()
    settle_axis(Z, z, user_emb, user_out, 0)
    settle_axis(X, x, user_emb, user_out, half * tile)
    own_ask.wait()
    pltpu.make_async_copy(request.at[rest], asked.at[rest], ask_came).wait()
    pltpu.make_async_copy(request.at[rest], asked.at[rest], ask_sent).wait()
    listed = pltpu.make_async_copy(asked, wanted, kept.at[10])
    listed.start()
    listed.wait()
    settle_axis(Y, y, item_emb, item_out, 0)
    for k in range(each):
        local = lax.rem(negatives[me * each + k], item_out.shape[0])
        stage[0, pl.ds(k, 1)] = item_out[pl.ds(local, 1)]
    chosen_negs[group, x, z] = stage[0, pl.ds(0, each)].astype(jnp.bfloat16)
    own = chosen_negs.at[group, x, z]
    first = [send(9 + s, own, own, {X: ahead(X, s)}) for s in steps]
    stores = [
        pltpu.make_async_copy(user_out, user_to, kept.at[12]),
        pltpu.make_async_copy(item_out, item_to, kept.at[13]),
    ]
    for copy in stores:
        copy.start()

    def pack(goals):
        for g, d in enumerate(goals):
            for k in range(each):
                stage[g, pl.ds(k, 1)] = user_out[pl.ds(wanted[d, 0, k], 1)]
                stage[g, pl.ds(each + k, 1)] = item_out[pl.ds(wanted[d, 0, each + k], 1)]
        for g, d in enumerate(goals):
            packs[d] = stage[g].astype(jnp.bfloat16)

    def give(group):
        goals = [other(s) for s in group]
        pack(goals)
        for d in goals:
            pltpu.make_async_remote_copy(
                packs.at[d], arrived.at[me], row_sent, row_came, device_id=coords(d)
            ).start()

    to_others(give)
    for copy in first:
        copy.wait()
    line = chosen_negs.at[group, :, z]
    second = [send(12 + s, line, line, {Z: ahead(Z, s)}) for s in steps]
    for copy in second:
        copy.wait()
    plane = chosen_negs.at[group]
    third = [send(16 + k, plane, plane, mate) for k, mate in enumerate(mates)]
    pack([me])
    mine = pltpu.make_async_copy(packs.at[me], arrived.at[me], kept.at[11])
    mine.start()
    mine.wait()
    pltpu.make_async_copy(packs.at[rest], arrived.at[rest], row_came).wait()
    pltpu.make_async_copy(packs.at[rest], arrived.at[rest], row_sent).wait()
    for copy in third:
        copy.wait()

    def picked(slot, first):
        rows = arrived[:, pl.ds(first, each)].reshape(devices * each, -1)
        hits = lax.broadcasted_iota(jnp.int32, (slot.shape[0], devices * each), 1) == slot[...]
        return jnp.dot(hits.astype(jnp.bfloat16), rows, preferred_element_type=jnp.float32)

    users = picked(user_slot, 0)
    chosen = picked(item_slot, each)
    positive[...] = jnp.sum(users * chosen, axis=1, keepdims=True)
    user_vec[...] = users.astype(jnp.bfloat16)
    negative_vec[...] = chosen_negs[...].reshape(devices * each, -1)
    for copy in stores:
        copy.wait()


def settle(over_x, over_z, items, user_emb, item_emb, request, user_slot, item_slot, negatives):
    side = items.shape[1:]
    embed = user_emb.shape[1]
    half, shard = over_x[0].shape[1], item_emb.shape[0] // side[0]
    items = items.reshape(SIDE, 2, shard, *side)
    devices, pairs = request.shape[0], user_slot.shape[0]
    each = negatives.shape[0] // devices
    many, one, low = (SIDE, half, *side), (half, *side), jnp.bfloat16
    return pl.pallas_call(
        functools.partial(settle_kernel, devices, each),
        name="settle",
        out_shape=(
            jax.ShapeDtypeStruct(user_emb.shape, jnp.float32),
            jax.ShapeDtypeStruct(item_emb.shape, jnp.float32),
            jax.ShapeDtypeStruct((pairs, embed), low),
            jax.ShapeDtypeStruct((pairs, 1), jnp.float32),
            jax.ShapeDtypeStruct((devices * each, embed), low),
        ),
        in_specs=[ANY] * 9 + [VMEM] * 3 + [SMEM],
        out_specs=(ANY, ANY, VMEM, VMEM, VMEM),
        scratch_shapes=[
            pltpu.VMEM(user_emb.shape, jnp.float32), pltpu.VMEM(item_emb.shape, jnp.float32),
            pltpu.VMEM(user_emb.shape, jnp.float32), pltpu.VMEM(item_emb.shape, jnp.float32),
            pltpu.VMEM((3, *many), low), pltpu.VMEM((3, *many), low),
            pltpu.VMEM((3, *one), low), pltpu.VMEM((3, *one), low),
            pltpu.VMEM((3, *one), low), pltpu.VMEM((3, *one), low),
            pltpu.VMEM((2, SIDE, shard, *side), low), pltpu.VMEM((3, shard, *side), low),
            pltpu.VMEM((3, shard, *side), low),
            pltpu.VMEM((devices, 1, 128), jnp.int32), pltpu.SMEM((devices, 1, 128), jnp.int32),
            pltpu.VMEM((8, 2 * each, embed), jnp.float32),
            pltpu.VMEM((devices, 2 * each, embed), low), pltpu.VMEM((devices, 2 * each, embed), low),
            pltpu.VMEM((2 * SIDE, SIDE, SIDE, each, embed), low),
            DMA((27,)), DMA((27,)), DMA((14,)), pltpu.SemaphoreType.REGULAR((2,)), DMA, DMA, DMA, DMA,
        ],
        compiler_params=pltpu.CompilerParams(
            collective_id=1, has_side_effects=True, vmem_limit_bytes=WHOLE
        ),
    )(*over_x, *over_z, items, user_emb, item_emb, request, user_slot, item_slot, negatives)


def last_kernel(user_vec, positive, negative_vec, users, items, terms, users_out, items_out):
    margin = lax.dot_general(
        user_vec[...], negative_vec[...], (((1,), (1,)), ((), ())), preferred_element_type=jnp.float32
    )
    terms[...] = jnp.log1p(jnp.exp(margin - positive[...]))
    users_out[...] = users[...]
    items_out[...] = items[...]


def last(user_vec, positive, negative_vec, users, items, steps=2):
    def block(array):
        return pl.BlockSpec((array.shape[0] // steps, array.shape[1]), lambda i: (i, 0))

    terms = jax.ShapeDtypeStruct((user_vec.shape[0], negative_vec.shape[0]), jnp.float32)
    return pl.pallas_call(
        last_kernel,
        name="last",
        grid=(steps,),
        out_shape=[terms] + [jax.ShapeDtypeStruct(array.shape, array.dtype) for array in (users, items)],
        in_specs=[block(user_vec), block(positive), pl.BlockSpec(negative_vec.shape, lambda i: (0, 0)), block(users), block(items)],
        out_specs=[block(terms), block(users), block(items)],
        compiler_params=pltpu.CompilerParams(vmem_limit_bytes=WHOLE),
    )(user_vec, positive, negative_vec, users, items)


def joined_kernel(*refs):
    for part, came, out in zip(refs[:4], refs[4:8], refs[8:]):
        for i in range(part.shape[1]):
            out[0, i] = (part[0, i].astype(jnp.float32) + came[0, i].astype(jnp.float32)).astype(out.dtype)


def joined(parts, relayed):
    block = (1, *parts[0].shape[1:])
    starts = (0, parts[0].shape[0] // 2) * 2
    spots = [pl.BlockSpec(block, lambda i, start=start: (start + i, 0, 0, 0)) for start in starts]
    return pl.pallas_call(
        joined_kernel,
        name="joined",
        grid=(parts[0].shape[0] // 2,),
        out_shape=[jax.ShapeDtypeStruct(part.shape, part.dtype) for part in parts],
        in_specs=spots + [pl.BlockSpec(block, lambda i: (i, 0, 0, 0))] * 4,
        out_specs=spots,
        input_output_aliases={k: k for k in range(4)},
        compiler_params=pltpu.CompilerParams(vmem_limit_bytes=WHOLE),
        cost_estimate=pl.CostEstimate(flops=2**20, bytes_accessed=6 * 2**20, transcendentals=0),
    )(*parts, *relayed)


def tile_kernel(width, depth, users, place, pieces, take, count_ref, rows, cols, vals, *refs):
    parts, outs, (acc, bufs, table, ready, sems, filled, emptied) = refs[:pieces], refs[pieces:-7], refs[-7:]
    total = acc.shape[0] - 1
    count = count_ref[0]
    chunks = (count + width - 1) // width

    def fetch(k, slot):
        return pltpu.make_async_copy(vals.at[pl.ds(k * width, width)], bufs.at[slot], sems.at[slot])

    for k in range(depth - 1):

        @pl.when(k < chunks)
        def _():
            fetch(k, k).start()

    copies = [
        pltpu.make_async_copy(part, table.at[pl.ds(start, part.shape[0])], filled)
        for part, start in place(parts)
    ]
    for copy in copies:
        copy.start()

    @pl.loop(0, total + 1)
    def _(i):
        acc[i] = jnp.zeros(acc.shape[1:], jnp.float32)

    pltpu.make_async_copy(table, table, filled).wait()

    @pl.loop(0, chunks)
    def _(k):
        slot = lax.rem(k, depth)
        ahead = k + depth - 1

        @pl.when(ahead < chunks)
        def _():
            fetch(ahead, lax.rem(ahead, depth)).start()

        fetch(k, slot).wait()
        products = []
        for t in range(width):
            spot = k * width + t
            tile = bufs[slot, t]
            if users:
                left, right, goal = tile, table[cols[spot]], rows[spot]
            else:
                left, right, goal = table[rows[spot]], tile, cols[spot]
            product = jnp.dot(left, right, preferred_element_type=jnp.float32)
            products.append((jnp.where(spot < count, goal, total), product))
        for goal, product in products:
            acc[goal] += product

    for out, start in take(outs):
        rows = pl.ds(start, out.shape[0])

        @pl.loop(0, out.shape[0])
        def _(i, start=start):
            tile = acc[start + i]
            ready[start + i] = (tile if users else tile.T).astype(jnp.bfloat16)

        pltpu.make_async_copy(ready.at[rows], out, emptied).start()
    pltpu.make_async_copy(ready, ready, emptied).wait()


def tile_terms(users, vals, rows, cols, count, parts, place, held, out_shapes, take, width=64, depth=3):
    slots, side, embed = *vals.shape[:2], parts[0].shape[-1]
    total = sum(shape[0] * (shape[1] if len(shape) == 4 else 1) for shape in out_shapes)
    return pl.pallas_call(
        functools.partial(tile_kernel, width, depth, users, place, len(parts), take),
        name="user_terms" if users else "item_terms",
        out_shape=[jax.ShapeDtypeStruct(shape, jnp.bfloat16) for shape in out_shapes],
        in_specs=[SMEM, SMEM, SMEM, ANY] + [ANY] * len(parts),
        out_specs=[ANY] * len(out_shapes),
        scratch_shapes=[
            pltpu.VMEM((total + 1, side, embed), jnp.float32),
            pltpu.VMEM((depth, width, side, side), jnp.bfloat16),
            pltpu.VMEM((held, side, embed), jnp.bfloat16),
            pltpu.VMEM((total, side, embed), jnp.bfloat16),
            DMA((depth,)),
            DMA,
            DMA,
        ],
        compiler_params=pltpu.CompilerParams(vmem_limit_bytes=WHOLE),
        cost_estimate=pl.CostEstimate(
            flops=slots * 2 * side * side * embed,
            bytes_accessed=2 * (vals.size + (held + total) * side * embed),
            transcendentals=0,
        ),
    )(count, rows, cols, vals, *parts)


def on_device(
    user_emb,
    item_emb,
    tile_vals,
    tile_rows,
    tile_cols,
    tile_count,
    pair_users,
    pair_items,
    negatives,
):
    row_count = lax.axis_size(ROW)
    col_count = lax.axis_size(COL)
    user_dev = user_emb.shape[2]
    item_dev = item_emb.shape[2]
    embed = user_emb.shape[3]
    side = tile_vals.shape[-1]
    user_each = user_dev // side
    half = user_each // 2
    slots = (tile_vals[0, 0], tile_rows[0, 0], tile_cols[0, 0], tile_count[0])

    devices = row_count * col_count
    user_rows, item_rows = user_emb.reshape(-1, embed), item_emb.reshape(-1, embed)
    item_tiles, x_low, x_high, z_low, z_high, user_slot, item_slot, request = first_gather(
        item_rows, user_rows, side, pair_users[None], pair_items[None], (user_dev, item_dev), devices
    )
    held = [(x_low, 0, 0, 0), (x_high, 0, 0, 1), (z_low, 0, 1, 0), (z_high, 0, 1, 1)]
    near = []
    for first in (True, False):
        for array, _, late, k in held:
            step = 1 if (k == 0) == first else -1
            moved = shifted(array, X if late else Z, step)
            near.append((moved, SIDE - 1 if step == -1 else 1, late, k))

    def item_places(refs):
        return [(refs[0], 0)]

    def item_takes(refs):
        for start in range(0, item_tiles.shape[0], 16):
            yield refs[0].at[pl.ds(start, 16)], start

    def dealt(refs):
        for late, axis in ((0, X), (1, Z)):
            own, up, down, low, high = refs[5 * late : 5 * late + 5]
            for step, to in ((0, own), (1, up), (3, down), (2, None)):
                goal = ahead(axis, step)
                for i in range(SIDE):
                    holder = i * SIDE + goal if late else goal * SIDE + i
                    ref = (low if i < 2 else high).at[i % 2] if to is None else to.at[i]
                    yield ref, holder * user_each + late * half

    many, few = (SIDE, half, side, embed), (SIDE // 2, half, side, embed)
    user_parts = tile_terms(
        True, *slots, [item_tiles], item_places, item_tiles.shape[0],
        [many, many, many, few, few] * 2, dealt,
    )
    relay = []
    for late, axis in ((0, X), (1, Z)):
        for k, step in ((3, 1), (4, -1)):
            relay.append(shifted(user_parts[5 * late + k], axis, step))
    far = []
    for array, back, late, k in near[:4]:
        sent_on = shifted(array, X if late else Z, 1 if back == 1 else -1)
        far.append((sent_on, 2, late, k))
    onward = joined([user_parts[k] for k in (1, 2, 6, 7)], relay)
    over_x, over_z = [user_parts[0]], [user_parts[5]]
    for k, (over, axis, step) in enumerate(((over_x, X, 1), (over_x, X, -1), (over_z, Z, 1), (over_z, Z, -1))):
        over.append(shifted(onward[k], axis, step))
    spread = held + near + far

    def user_places(refs):
        for ref, (array, back, late, k) in zip(refs, spread):
            at = lax.rem(lax.axis_index(X if late else Z) + SIDE - back, SIDE)
            for i in range(SIDE):
                holder = at * SIDE + i if late else i * SIDE + at
                yield ref.at[i], holder * user_each + late * half + k * (half // 2)

    (item_part,) = tile_terms(
        False, *slots, [part[0] for part in spread], user_places, user_each * col_count,
        [item_tiles.shape], item_takes,
    )
    user_final, item_final, user_vec, positive, negative_vec = settle(
        over_x, over_z, item_part, user_rows, item_rows, request, user_slot, item_slot, negatives
    )
    bpr_terms, user_final, item_final = last(user_vec, positive, negative_vec, user_final, item_final)
    return (user_final.reshape(user_emb.shape), item_final.reshape(item_emb.shape), bpr_terms)


def solution(mesh):
    torus = Mesh(mesh.devices.reshape(4, 2, 4, 4), ("row_0", "row_1", "col_0", "col_1"))

    return jax.shard_map(
        on_device,
        mesh=torus,
        in_specs=(
            P(ROW, COL, None, None),
            P(COL, ROW, None, None),
            P(ROW, COL, None, None, None),
            P(ROW, COL, None),
            P(ROW, COL, None),
            P(ROW, COL),
            P(ROW_COL),
            P(ROW_COL),
            P(),
        ),
        out_specs=(P(ROW, COL, None, None), P(COL, ROW, None, None), P(ROW_COL, None)),
        check_vma=False,
    )
```
